32 devices in a mesh: section: 4 (over z), dp: 8 (over y, x, core).
Axes of the slice: x: 2, y: 2, z: 4, core: 2. Of those that a mesh axis runs over, the one named last changes fastest.
Arguments:
- acts: bfloat16 [4, 4, 8, 12, 16, 512], P('section', None, 'dp'), may hold values from -6 to 6
- out_grad: bfloat16 [4, 8, 12, 16, 512], P(None, 'dp'), may hold values from -6 to 6
- depth_kernel: bfloat16 [4, 3, 3, 512], P('section'), may hold values from -2 to 2
- point_weight: bfloat16 [4, 512, 512], P('section'), may hold values from -0.25 to 0.25
- bn_gain: float32 [4, 512], P('section'), may hold values from 0.15 to 0.45
Outputs:
- act_grad: bfloat16 [4, 4, 8, 12, 16, 512], P('section', None, 'dp')
- point_grad: float32 [4, 512, 512], P('section')
- kernel_grad: float32 [4, 3, 3, 512], P('section')
- gain_grad: float32 [4, 512], P('section')
- bias_grad: float32 [4, 512], P('section')
The draws below stay inside these ranges and needn't reach their ends.
All inputs are finite; a program needn't handle non-finite values.
Results may differ from the reference program's by a relative error of at most 0.025.
Values may be sent and summed in bfloat16 or wider, within the bound.
No kernel may reach another device: no remote copies, remote signals or barrier semaphores. Data moves between devices by JAX's collectives and lax.ppermute only.
A program may use at most 64 MiB of HBM per device.

```python
import jax
import jax.numpy as jnp
from jax import lax

CHANNELS = 512
HEIGHT = 12
WIDTH = 16
MICRO = 4
SECTIONS = 4
IMAGES = 8


def steps_of(key, dims, cuts, low, top_value):
    level = 1.0
    for axis_at, parts in cuts:
        heights = jax.random.uniform(jax.random.fold_in(jax.random.fold_in(key, 6), axis_at), (parts,), jnp.float32, low / len(cuts), top_value / len(cuts))
        level = level * jnp.repeat(jnp.exp(heights), dims[axis_at] // parts).reshape((-1,) + (1,) * (len(dims) - 1 - axis_at))
    return level


def centred(rng, shape, scale, limit, pieces=(), kind=jnp.bfloat16):
    result = scale * jax.random.normal(rng, shape, jnp.float32)
    if pieces:
        result = result * steps_of(rng, shape, pieces, -0.22, 0.18)
    return jnp.clip(result, -limit, limit).astype(kind)


def setup_inputs(seed: int = 0) -> dict:
    key_list = jax.random.split(jax.random.key(seed), 6)
    return {
        "acts": centred(key_list[0], (SECTIONS, MICRO, IMAGES, HEIGHT, WIDTH, CHANNELS), 1.0, 6.0, ((0, 4), (2, 8))),
        "out_grad": centred(key_list[1], (MICRO, IMAGES, HEIGHT, WIDTH, CHANNELS), 1.0, 6.0, ((1, 8),)),
        "depth_kernel": centred(key_list[2], (SECTIONS, 3, 3, CHANNELS), 9 ** -0.5, 2.0, ((0, 4),)),
        "point_weight": centred(key_list[3], (SECTIONS, CHANNELS, CHANNELS), CHANNELS ** -0.5, 0.25, ((0, 4),)),
        "bn_gain": jnp.clip(0.15 + 0.29999998 * jax.random.uniform(key_list[4], (SECTIONS, CHANNELS), jnp.float32) ** steps_of(key_list[4], (SECTIONS, CHANNELS), ((0, 4),), -0.2, 0.2), 0.15, 0.45),
    }


epsilon = 1e-05

def depthwise(active, kernel):
    padded = jnp.pad(active, ((0, 0), (1, 1), (1, 1), (0, 0)))
    height, width = (active.shape[1], active.shape[2])
    summed = jnp.zeros(active.shape, jnp.float32)
    for row_off in range(3):
        for col_off in range(3):
            summed = summed + kernel[row_off, col_off] * padded[:, row_off:row_off + height, col_off:col_off + width]
    return summed

def depthwise_back(grad, kernel):
    padded = jnp.pad(grad, ((0, 0), (1, 1), (1, 1), (0, 0)))
    height, width = (grad.shape[1], grad.shape[2])
    summed = jnp.zeros(grad.shape, jnp.float32)
    for row_off in range(3):
        for col_off in range(3):
            summed = summed + kernel[row_off, col_off] * padded[:, 2 - row_off:2 - row_off + height, 2 - col_off:2 - col_off + width]
    return summed

def kernel_terms(active, grad):
    padded = jnp.pad(active, ((0, 0), (1, 1), (1, 1), (0, 0)))
    height, width = (active.shape[1], active.shape[2])
    table = []
    for row_off in range(3):
        line = []
        for col_off in range(3):
            line.append(lax.optimization_barrier(jnp.sum(padded[:, row_off:row_off + height, col_off:col_off + width] * grad, axis=(0, 1, 2))))
        table.append(jnp.stack(line))
    return jnp.stack(table)

def reference(acts, out_grad, depth_kernel, point_weight, bn_gain):
    count = IMAGES * HEIGHT * WIDTH
    shape = (IMAGES, HEIGHT, WIDTH, CHANNELS)
    below = None
    grads_all, points_all, kernels_all, gains_all, biases_all = ([], [], [], [], [])
    for section in reversed(range(SECTIONS)):
        kernel = depth_kernel[section].astype(jnp.float32)
        weight = point_weight[section]
        gain = bn_gain[section]
        point_acc = jnp.zeros((CHANNELS, CHANNELS), jnp.float32)
        kernel_acc = jnp.zeros((3, 3, CHANNELS), jnp.float32)
        gain_acc = jnp.zeros((CHANNELS,), jnp.float32)
        bias_acc = jnp.zeros((CHANNELS,), jnp.float32)
        results = []
        for micro in range(MICRO):
            inputs = acts[section, micro]
            active = jnp.maximum(inputs.astype(jnp.float32), 0.0)
            depth_out = depthwise(active, kernel).astype(jnp.bfloat16).reshape(-1, CHANNELS)
            pre_norm = jnp.dot(depth_out, weight, preferred_element_type=jnp.float32)
            center = lax.optimization_barrier(jnp.sum(pre_norm, axis=0)) / count
            square = lax.optimization_barrier(jnp.sum(pre_norm * pre_norm, axis=0)) / count
            inv_std = lax.rsqrt(square - center * center + epsilon)
            normed = (pre_norm - center) * inv_std
            if section == SECTIONS - 1:
                upstream = out_grad[micro]
            else:
                upstream = below[micro]
            upstream = upstream.astype(jnp.float32).reshape(-1, CHANNELS)
            sum_grad = lax.optimization_barrier(jnp.sum(upstream, axis=0))
            sum_cross = lax.optimization_barrier(jnp.sum(upstream * normed, axis=0))
            gain_acc = gain_acc + sum_cross
            bias_acc = bias_acc + sum_grad
            pre_grad = (gain * inv_std * (upstream - sum_grad / count - normed * sum_cross / count)).astype(jnp.bfloat16)
            point_acc = point_acc + jnp.dot(depth_out.T, pre_grad, preferred_element_type=jnp.float32)
            depth_grad = jnp.dot(pre_grad, weight.T, preferred_element_type=jnp.float32).reshape(shape)
            kernel_acc = kernel_acc + kernel_terms(active, depth_grad)
            back = depthwise_back(depth_grad, kernel)
            input_grad = upstream.reshape(shape) + jnp.where(inputs > 0, back, 0.0)
            results.append(input_grad.astype(jnp.bfloat16))
        below = results
        grads_all.append(jnp.stack(results))
        points_all.append(point_acc)
        kernels_all.append(kernel_acc)
        gains_all.append(gain_acc)
        biases_all.append(bias_acc)
    act_grad = jnp.stack(grads_all[::-1])
    point_grad = jnp.stack(points_all[::-1])
    kernel_grad = jnp.stack(kernels_all[::-1])
    gain_grad = jnp.stack(gains_all[::-1])
    bias_grad = jnp.stack(biases_all[::-1])
    return (act_grad, point_grad, kernel_grad, gain_grad, bias_grad)
```

```python
import functools

import jax
import jax.numpy as jnp
from jax import lax
from jax.experimental import pallas as pl
from jax.experimental.pallas import tpu as pltpu
from jax.sharding import PartitionSpec as P

epsilon = 1e-05
LANES = 128
F32 = jnp.float32
BF16 = jnp.bfloat16

GROUP = 2
PARAMS = pltpu.CompilerParams(vmem_limit_bytes=16 << 20)


def cyclic(v, width):
    col = lax.broadcasted_iota(jnp.int32, v.shape, 0)
    before = jnp.where(col == 0, 0.0, pltpu.roll(v, 1, 0))
    after = jnp.where(col == width - 1, 0.0, pltpu.roll(v, width - 1, 0))
    return before, v, after


def lane_loop(channels, work):
    def step(i, carry):
        work(pl.ds(pl.multiple_of(i * LANES, LANES), LANES))
        return carry

    lax.fori_loop(0, channels // LANES, step, 0)


def kernel_rows(kernel_ref, lanes):
    return [[kernel_ref[i, j : j + 1, lanes].astype(F32) for j in range(3)] for i in range(3)]


def col_sum(v):
    return jnp.sum(v, axis=0, keepdims=True)


def forward_kernel(height, width, group, x_ref, og_ref, kernel_ref, w_ref, *rest):
    depth_ref, pre_ref, raw_ref = rest[:3]
    copies = rest[3:-1]
    pre_s = rest[-1]
    channels = x_ref.shape[-1]

    def conv(lanes):
        taps = kernel_rows(kernel_ref, lanes)

        def parts(h):
            v = jnp.maximum(x_ref[0, h * width : (h + 1) * width, lanes].astype(F32), 0.0)
            cols = cyclic(v, width)
            return [sum(taps[i][j] * cols[j] for j in range(3)) for i in range(3)]

        window = [None, parts(0), None]
        for h in range(height):
            window[2] = parts(h + 1) if h + 1 < height else None
            total = window[1][1]
            if window[0] is not None:
                total = total + window[0][0]
            if window[2] is not None:
                total = total + window[2][2]
            depth_ref[0, h * width : (h + 1) * width, lanes] = total.astype(BF16)
            window = [window[1], window[2], None]

    lane_loop(channels, conv)
    pre_s[...] = jnp.dot(depth_ref[0], w_ref[...], preferred_element_type=F32)

    def sums(lanes):
        p = pre_s[:, lanes]
        g = og_ref[0, :, lanes].astype(F32)
        pre_ref[0, :, lanes] = p.astype(BF16)
        raw_ref[0, 0:1, lanes] = col_sum(p)
        raw_ref[0, 1:2, lanes] = col_sum(p * p)
        raw_ref[0, 2:3, lanes] = col_sum(g)
        raw_ref[0, 3:4, lanes] = col_sum(g * p)

    lane_loop(channels, sums)
    for i in range(len(copies)):

        @pl.when(pl.program_id(0) // group == i)
        def _():
            copies[i][0] = pre_ref[0]


def forward(x, og, kernel, weight, height, width, group):
    micros, rows, channels = x.shape
    block = pl.BlockSpec((1, rows, channels), lambda m: (m, 0, 0))

    def own(i):
        return pl.BlockSpec(
            (1, rows, channels), lambda m: (jnp.clip(m - i * group, 0, group - 1), 0, 0)
        )

    groups = micros // group
    return pl.pallas_call(
        functools.partial(forward_kernel, height, width, group),
        grid=(micros,),
        in_specs=[
            block,
            block,
            pl.BlockSpec(kernel.shape, lambda m: (0, 0, 0)),
            pl.BlockSpec(weight.shape, lambda m: (0, 0)),
        ],
        out_specs=[block, block, pl.BlockSpec((1, 4, channels), lambda m: (m, 0, 0))]
        + [own(i) for i in range(groups)],
        out_shape=[
            jax.ShapeDtypeStruct(x.shape, BF16),
            jax.ShapeDtypeStruct(x.shape, BF16),
            jax.ShapeDtypeStruct((micros, 4, channels), F32),
        ]
        + [jax.ShapeDtypeStruct((group, rows, channels), BF16)] * groups,
        scratch_shapes=[pltpu.VMEM((rows, channels), F32)],
        compiler_params=PARAMS,
        name="forward",
    )(x, og, kernel, weight)


def chunk_of(t, sections, groups, ids):
    at = t - (sections - 1) + ids[0]
    inside = jnp.clip(at, 0, groups - 1)
    return inside, at == inside


def turn_kernel(height, width, count, first, sections, ids, og_ref, raw_ref, gain_ref, pre_ref, x_ref, w_ref, kernel_ref, *rest):
    if first:
        recv_ref = tot_ref = None
        outs = rest
    else:
        recv_ref, tot_ref = rest[:2]
        outs = rest[4:]
    u_out, total_out, act_out, pg_out, dg_out, rows_s, dg_s = outs
    channels = x_ref.shape[-1]
    top = ids[0] == sections - 1

    def upstream(line, lanes):
        own = og_ref[0, line, lanes]
        return (own if first else jnp.where(top, own, recv_ref[0, line, lanes])).astype(F32)

    def reduced(row):
        own = raw_ref[0, 2 + row : 3 + row, :]
        return own if first else jnp.where(top, own, tot_ref[0, row : row + 1, :])

    inverse = 1.0 / count
    center = raw_ref[0, 0:1, :] * inverse
    square = raw_ref[0, 1:2, :] * inverse
    inv = lax.rsqrt(square - center * center + epsilon)
    sum_grad = reduced(0)
    sum_cross = inv * (reduced(1) - center * sum_grad)
    total_out[0, 0:1, :] = sum_cross
    total_out[0, 1:2, :] = sum_grad
    scale = gain_ref[...] * inv
    slope = -scale * inv * sum_cross * inverse
    rows_s[0:1, :] = scale
    rows_s[1:2, :] = slope
    rows_s[2:3, :] = -scale * sum_grad * inverse - slope * center

    def grads(lanes):
        u = upstream(slice(None), lanes)
        pre = pre_ref[0, :, lanes].astype(F32)
        pg_out[0, :, lanes] = (rows_s[0:1, lanes] * u + rows_s[1:2, lanes] * pre + rows_s[2:3, lanes]).astype(BF16)

    lane_loop(channels, grads)
    dg_s[...] = lax.dot_general(
        pg_out[0], w_ref[...], (((1,), (1,)), ((), ())), preferred_element_type=F32
    )

    def conv(lanes):
        taps = kernel_rows(kernel_ref, lanes)

        def parts(h):
            v = dg_s[h * width : (h + 1) * width, lanes]
            dg_out[0, h * width : (h + 1) * width, lanes] = v.astype(BF16)
            cols = cyclic(v, width)
            return [sum(taps[i][2 - j] * cols[j] for j in range(3)) for i in range(3)]

        window = [None, parts(0), None]
        for h in range(height):
            window[2] = parts(h + 1) if h + 1 < height else None
            total = window[1][1]
            if window[0] is not None:
                total = total + window[0][2]
            if window[2] is not None:
                total = total + window[2][0]
            window = [window[1], window[2], None]
            line = slice(h * width, (h + 1) * width)
            x = x_ref[0, line, lanes].astype(F32)
            fresh = (upstream(line, lanes) + jnp.where(x > 0.0, total, 0.0)).astype(BF16)
            u_out[0, line, lanes] = fresh
            act_out[0, line, lanes] = fresh

    lane_loop(channels, conv)


def turn(t, sections, ids, og, raw, gain, pre, x, weight, kernel, carried, height, width, count, group):
    micros, rows, channels = x.shape
    groups = micros // group

    def inside(i, s):
        return chunk_of(t, sections, groups, s)[0] * group + i

    def kept(i, s):
        at, valid = chunk_of(t, sections, groups, s)
        return jnp.where(valid, at * group + i, micros)

    slot = pl.BlockSpec((1, rows, channels), lambda i, s: (inside(i, s), 0, 0))
    keep = pl.BlockSpec((1, rows, channels), lambda i, s: (kept(i, s), 0, 0))
    each = pl.BlockSpec((1, rows, channels), lambda i, s: (i, 0, 0))
    pair = pl.BlockSpec((1, 2, channels), lambda i, s: (i, 0, 0))
    hbm = pl.BlockSpec(memory_space=pl.ANY)
    first = not carried
    held = jax.ShapeDtypeStruct((micros + 1, rows, channels), BF16)
    sent = jax.ShapeDtypeStruct((group, rows, channels), BF16)
    return pl.pallas_call(
        functools.partial(turn_kernel, height, width, count, first, sections),
        grid_spec=pltpu.PrefetchScalarGridSpec(
            num_scalar_prefetch=1,
            grid=(group,),
            in_specs=[
                slot,
                pl.BlockSpec((1, 4, channels), lambda i, s: (inside(i, s), 0, 0)),
                pl.BlockSpec((1, channels), lambda i, s: (0, 0)),
                slot,
                slot,
                pl.BlockSpec(weight.shape, lambda i, s: (0, 0)),
                pl.BlockSpec(kernel.shape, lambda i, s: (0, 0, 0)),
            ]
            + ([] if first else [each, pair, hbm, hbm]),
            out_specs=[each, pair, keep, keep, each],
            scratch_shapes=[
                pltpu.VMEM((8, channels), F32),
                pltpu.VMEM((rows, channels), F32),
            ],
        ),
        out_shape=[sent, jax.ShapeDtypeStruct((group, 2, channels), F32), held, held, sent],
        input_output_aliases={} if first else {10: 2, 11: 3},
        compiler_params=PARAMS,
        name="turn",
    )(ids, og, raw, gain, pre, x, weight, kernel, *carried)


def cross_kernel(t, sections, groups, ids, u_ref, *rest):
    nexts, out = rest[:-1], rest[-1]
    channels = u_ref.shape[-1]
    at = chunk_of(t, sections, groups, ids)[0]

    def sums(lanes):
        u = u_ref[0, :, lanes].astype(F32)
        pre = nexts[0][0, :, lanes]
        for i in range(1, groups):
            pre = jnp.where(at == i, nexts[i][0, :, lanes], pre)
        out[0, 0:1, lanes] = col_sum(u)
        out[0, 1:2, lanes] = col_sum(u * pre.astype(F32))

    lane_loop(channels, sums)


def cross(t, sections, ids, u, nexts):
    group, rows, channels = u.shape
    each = pl.BlockSpec((1, rows, channels), lambda i, s: (i, 0, 0))
    return pl.pallas_call(
        functools.partial(cross_kernel, t, sections, len(nexts)),
        grid_spec=pltpu.PrefetchScalarGridSpec(
            num_scalar_prefetch=1,
            grid=(group,),
            in_specs=[each] * (1 + len(nexts)),
            out_specs=pl.BlockSpec((1, 2, channels), lambda i, s: (i, 0, 0)),
        ),
        out_shape=jax.ShapeDtypeStruct((group, 2, channels), F32),
        compiler_params=PARAMS,
        name="cross",
    )(ids, u, *nexts)


def terms_kernel(t, sections, groups, height, width, first, ids, x_ref, dg_ref, total_ref, *rest):
    acc_out, sums_out = rest[-2:]
    channels = x_ref.shape[-1]
    valid = chunk_of(t, sections, groups, ids)[1]

    @pl.when(pl.program_id(0) == 0)
    def _():
        acc_out[...] = jnp.zeros_like(acc_out) if first else rest[0][...]
        sums_out[...] = jnp.zeros_like(sums_out) if first else rest[1][...]

    sums_out[...] += jnp.where(valid, total_ref[0], 0.0)

    def terms(lanes):
        acc = [[None] * 3 for _ in range(3)]
        grads = [None] + [dg_ref[0, h * width : (h + 1) * width, lanes].astype(F32) for h in range(height)] + [None]
        for h in range(height):
            v = jnp.maximum(x_ref[0, h * width : (h + 1) * width, lanes].astype(F32), 0.0)
            cols = cyclic(v, width)
            for i in range(3):
                g = grads[h + 2 - i]
                if g is None:
                    continue
                for j in range(3):
                    p = cols[j] * g
                    acc[i][j] = p if acc[i][j] is None else acc[i][j] + p
        for i in range(3):
            for j in range(3):
                row = slice(3 * i + j, 3 * i + j + 1)
                acc_out[row, lanes] += jnp.where(valid, col_sum(acc[i][j]), 0.0)

    lane_loop(channels, terms)


def terms(t, sections, ids, x, dg, total, carried, height, width):
    micros, rows, channels = x.shape
    group = dg.shape[0]
    groups = micros // group
    flat = lambda n: pl.BlockSpec((n, channels), lambda i, s: (0, 0))
    return pl.pallas_call(
        functools.partial(terms_kernel, t, sections, groups, height, width, not carried),
        grid_spec=pltpu.PrefetchScalarGridSpec(
            num_scalar_prefetch=1,
            grid=(group,),
            in_specs=[
                pl.BlockSpec(
                    (1, rows, channels),
                    lambda i, s: (chunk_of(t, sections, groups, s)[0] * group + i, 0, 0),
                ),
                pl.BlockSpec((1, rows, channels), lambda i, s: (i, 0, 0)),
                pl.BlockSpec((1, 2, channels), lambda i, s: (i, 0, 0)),
            ]
            + ([flat(16), flat(2)] if carried else []),
            out_specs=[flat(16), flat(2)],
        ),
        out_shape=[
            jax.ShapeDtypeStruct((16, channels), F32),
            jax.ShapeDtypeStruct((2, channels), F32),
        ],
        compiler_params=PARAMS,
        name="terms",
    )(ids, x, dg, total, *carried)


def product_kernel(micros, half, where_ref, depth_ref, pg_ref, acc_ref, keep_out, send_out, total):
    step = pl.program_id(0)
    fresh = lax.dot_general(
        depth_ref[0], pg_ref[0], (((0,), (0,)), ((), ())), preferred_element_type=F32
    )

    @pl.when(step == 0)
    def _():
        total[...] = fresh

    @pl.when(step > 0)
    def _():
        total[...] += fresh

    @pl.when(step == micros - 1)
    def _():
        core = where_ref[1] % 2
        keep_out[...] = total[pl.ds(pl.multiple_of(core * half, half), half), :]
        other = pl.multiple_of((1 - core) * half, half)
        send_out[0:half, :] = total[pl.ds(other, half), :].astype(BF16)
        send_out[half : half + 16, :] = acc_ref[...].astype(BF16)


def product(where, depth, pg, acc):
    micros, rows, channels = depth.shape
    half = channels // 2
    block = pl.BlockSpec((1, rows, channels), lambda m, s: (m, 0, 0))
    return pl.pallas_call(
        functools.partial(product_kernel, micros, half),
        grid_spec=pltpu.PrefetchScalarGridSpec(
            num_scalar_prefetch=1,
            grid=(micros,),
            in_specs=[block, block, pl.BlockSpec((16, channels), lambda m, s: (0, 0))],
            out_specs=[
                pl.BlockSpec((half, channels), lambda m, s: (0, 0)),
                pl.BlockSpec((half + 16, channels), lambda m, s: (0, 0)),
            ],
            scratch_shapes=[pltpu.VMEM((channels, channels), F32)],
        ),
        out_shape=[
            jax.ShapeDtypeStruct((half, channels), F32),
            jax.ShapeDtypeStruct((half + 16, channels), BF16),
        ],
        compiler_params=PARAMS,
        name="product",
    )(where, depth, pg, acc)


def split_kernel(chips, chunk, where_ref, keep_ref, sent_ref, recv_ref, own_out, *outs):
    half = chips * chunk
    chip = where_ref[1] // 2
    table = sent_ref[half : half + 16, :].astype(F32) + recv_ref[half : half + 16, :].astype(F32)
    for k in range(chips):
        at = pl.multiple_of((chip ^ k) * chunk, chunk)
        piece = keep_ref[pl.ds(at, chunk), :] + recv_ref[pl.ds(at, chunk), :].astype(F32)
        if k == 0:
            own_out[0:chunk, :] = piece
            own_out[chunk : chunk + 16, :] = table.astype(BF16).astype(F32)
        else:
            outs[k - 1][0:chunk, :] = piece.astype(BF16)
            outs[k - 1][chunk : chunk + 16, :] = table.astype(BF16)


def split(where, keep, sent, recv, chips):
    half, channels = keep.shape
    chunk = half // chips
    vmem = pl.BlockSpec(memory_space=pltpu.VMEM)
    return pl.pallas_call(
        functools.partial(split_kernel, chips, chunk),
        in_specs=[pl.BlockSpec(memory_space=pltpu.SMEM), vmem, vmem, vmem],
        out_specs=[vmem] * chips,
        out_shape=[jax.ShapeDtypeStruct((chunk + 16, channels), F32)]
        + [jax.ShapeDtypeStruct((chunk + 16, channels), BF16)] * (chips - 1),
        compiler_params=PARAMS,
        name="split",
    )(where, keep, sent, recv)


def merge_kernel(chunk, own_ref, *refs):
    parts = [own_ref[...]] + [r[...].astype(F32) for r in refs[:-2]]
    while len(parts) > 1:
        parts = [a + b for a, b in zip(parts[::2], parts[1::2])]
    refs[-2][...] = parts[0][0:chunk, :].astype(BF16)
    refs[-1][...] = parts[0][chunk:, :]


def merge(own, recvs):
    chunk, channels = own.shape[0] - 16, own.shape[1]
    vmem = pl.BlockSpec(memory_space=pltpu.VMEM)
    return pl.pallas_call(
        functools.partial(merge_kernel, chunk),
        in_specs=[vmem] * (1 + len(recvs)),
        out_specs=[vmem] * 2,
        out_shape=[
            jax.ShapeDtypeStruct((chunk, channels), BF16),
            jax.ShapeDtypeStruct((16, channels), F32),
        ],
        compiler_params=PARAMS,
        name="merge",
    )(own, *recvs)


def gather_kernel(chunk, where_ref, *refs):
    for k, ref in enumerate(refs[:-1]):
        at = pl.multiple_of((where_ref[1] // 2 ^ k) * chunk, chunk)
        refs[-1][pl.ds(at, chunk), :] = ref[...]


def gather(where, parts):
    chunk, channels = parts[0].shape
    vmem = pl.BlockSpec(memory_space=pltpu.VMEM)
    return pl.pallas_call(
        functools.partial(gather_kernel, chunk),
        in_specs=[pl.BlockSpec(memory_space=pltpu.SMEM)] + [vmem] * len(parts),
        out_specs=vmem,
        out_shape=jax.ShapeDtypeStruct((chunk * len(parts), channels), BF16),
        compiler_params=PARAMS,
        name="gather",
    )(where, *parts)


def widen_kernel(half, where_ref, own_ref, recv_ref, out_ref):
    core = where_ref[1] % 2
    out_ref[0, pl.ds(pl.multiple_of(core * half, half), half), :] = own_ref[...].astype(F32)
    out_ref[0, pl.ds(pl.multiple_of((1 - core) * half, half), half), :] = recv_ref[...].astype(F32)


def widen(where, own, recv):
    half, channels = own.shape
    vmem = pl.BlockSpec(memory_space=pltpu.VMEM)
    return pl.pallas_call(
        functools.partial(widen_kernel, half),
        in_specs=[pl.BlockSpec(memory_space=pltpu.SMEM), vmem, vmem],
        out_specs=vmem,
        out_shape=jax.ShapeDtypeStruct((1, 2 * half, channels), F32),
        compiler_params=PARAMS,
        name="widen",
    )(where, own, recv)


def tree(parts):
    while len(parts) > 1:
        parts = [a + b for a, b in zip(parts[::2], parts[1::2])]
    return parts[0]


def body(acts, out_grad, depth_kernel, point_weight, bn_gain):
    sections = lax.axis_size("section")
    replicas = lax.axis_size("dp")
    micros, images, height, width, channels = acts.shape[1:]
    rows = images * height * width
    count = rows * replicas
    chips = replicas // 2
    group = GROUP if micros % GROUP == 0 else 1
    turns = sections + micros // group - 1
    x = acts.reshape(micros, rows, channels)
    og = out_grad.reshape(micros, rows, channels)
    kernel = depth_kernel[0]
    weight = point_weight[0]
    gain = bn_gain
    ids = jnp.stack([lax.axis_index("section"), lax.axis_index("dp")]).astype(jnp.int32)

    def swap(v, k):
        return lax.ppermute(v, "dp", [(i, i ^ k) for i in range(replicas)])

    def down(v):
        return lax.ppermute(v, "section", [(i, i - 1) for i in range(1, sections)])

    def up(v):
        return lax.ppermute(v, "section", [(i, i + 1) for i in range(sections - 1)])

    def everywhere(v):
        v = v + swap(v, 1)
        return tree([v] + [swap(v, k) for k in range(2, replicas, 2)])

    out = forward(x, og, kernel, weight, height, width, group)
    depth, pre, raw = out[:3]
    nexts = [up(out[3])]
    raw = everywhere(raw)
    later, raw = lax.optimization_barrier((out[4:], raw))
    nexts += [up(p) for p in later]

    carried, collected = (), ()
    for t in range(turns):
        fresh, total, act, pg, dg = turn(
            t, sections, ids, og, raw, gain, pre, x, weight, kernel, carried,
            height, width, count, group,
        )
        if t + 1 < turns:
            recv = down(fresh)
            tot = down(everywhere(cross(t, sections, ids, fresh, nexts)))
            carried = (recv, tot, act, pg)
        collected = terms(t, sections, ids, x, dg, total, collected, height, width)
        gain, collected = lax.optimization_barrier((gain, collected))
    acc, sums = collected
    keep, send = product(ids, depth, pg, acc)
    got = split(ids, keep, send, swap(send, 1), chips)
    chunk, table = merge(got[0], [swap(v, 2 * k) for k, v in enumerate(got[1:], 1)])
    half = gather(ids, [chunk] + [swap(chunk, 2 * k) for k in range(1, chips)])
    point = widen(ids, half, swap(half, 1))
    act = act[:micros].reshape(acts.shape)
    return (act, point, table[:9].reshape(1, 3, 3, channels), sums[0:1], sums[1:2])


def solution(mesh):
    return jax.shard_map(
        body,
        mesh=mesh,
        in_specs=(
            P("section", None, "dp", None, None, None),
            P(None, "dp", None, None, None),
            P("section", None, None, None),
            P("section", None, None),
            P("section", None),
        ),
        out_specs=(
            P("section", None, "dp", None, None, None),
            P("section", None, None),
            P("section", None, None, None),
            P("section", None),
            P("section", None),
        ),
        check_vma=False,
    )
```

```python
import functools

import jax
import jax.numpy as jnp
from jax import lax
from jax.experimental import pallas as pl
from jax.experimental.pallas import tpu as pltpu
from jax.sharding import PartitionSpec as P

epsilon = 1e-05
LANES = 128
F32 = jnp.float32
BF16 = jnp.bfloat16

GROUP = 2
PARAMS = pltpu.CompilerParams(vmem_limit_bytes=16 << 20)


def cyclic(v, width):
    col = lax.broadcasted_iota(jnp.int32, v.shape, 0)
    before = jnp.where(col == 0, 0.0, pltpu.roll(v, 1, 0))
    after = jnp.where(col == width - 1, 0.0, pltpu.roll(v, width - 1, 0))
    return before, v, after


def lane_loop(channels, work):
    def step(i, carry):
        work(pl.ds(pl.multiple_of(i * LANES, LANES), LANES))
        return carry

    lax.fori_loop(0, channels // LANES, step, 0)


def kernel_rows(kernel_ref, lanes):
    return [[kernel_ref[i, j : j + 1, lanes].astype(F32) for j in range(3)] for i in range(3)]


def col_sum(v):
    return jnp.sum(v, axis=0, keepdims=True)


VMEM = pl.BlockSpec(memory_space=pltpu.VMEM)
SMEM = pl.BlockSpec(memory_space=pltpu.SMEM)
ANY = pl.BlockSpec(memory_space=pl.ANY)


def forward_kernel(height, width, x_ref, og_ref, kernel_ref, w_ref, *rest):
    depth_ref, pre_ref, raw_ref, copy_ref, pre_s = rest[-5:]
    channels = x_ref.shape[-1]

    def conv(lanes):
        taps = kernel_rows(kernel_ref, lanes)

        def parts(h):
            v = jnp.maximum(x_ref[0, h * width : (h + 1) * width, lanes].astype(F32), 0.0)
            cols = cyclic(v, width)
            return [sum(taps[i][j] * cols[j] for j in range(3)) for i in range(3)]

        window = [None, parts(0), None]
        for h in range(height):
            window[2] = parts(h + 1) if h + 1 < height else None
            total = window[1][1]
            if window[0] is not None:
                total = total + window[0][0]
            if window[2] is not None:
                total = total + window[2][2]
            depth_ref[0, h * width : (h + 1) * width, lanes] = total.astype(BF16)
            window = [window[1], window[2], None]

    lane_loop(channels, conv)
    pre_s[...] = jnp.dot(depth_ref[0], w_ref[...], preferred_element_type=F32)

    def sums(lanes):
        p = pre_s[:, lanes]
        g = og_ref[0, :, lanes].astype(F32)
        short = p.astype(BF16)
        pre_ref[0, :, lanes] = short
        copy_ref[0, :, lanes] = short
        raw_ref[0, 0:1, lanes] = col_sum(p)
        raw_ref[0, 1:2, lanes] = col_sum(p * p)
        raw_ref[0, 2:3, lanes] = col_sum(g)
        raw_ref[0, 3:4, lanes] = col_sum(g * p)

    lane_loop(channels, sums)


def forward(part, x, og, kernel, weight, held, height, width, group):
    micros, rows, channels = x.shape
    block = pl.BlockSpec((1, rows, channels), lambda m: (m + part * group, 0, 0))
    return pl.pallas_call(
        functools.partial(forward_kernel, height, width),
        grid=(group,),
        in_specs=[
            block,
            block,
            pl.BlockSpec(kernel.shape, lambda m: (0, 0, 0)),
            pl.BlockSpec(weight.shape, lambda m: (0, 0)),
        ]
        + [ANY] * len(held),
        out_specs=[
            block,
            block,
            pl.BlockSpec((1, 4, channels), lambda m: (m + part * group, 0, 0)),
            pl.BlockSpec((1, rows, channels), lambda m: (m, 0, 0)),
        ],
        out_shape=[
            jax.ShapeDtypeStruct(x.shape, BF16),
            jax.ShapeDtypeStruct(x.shape, BF16),
            jax.ShapeDtypeStruct((micros, 4, channels), F32),
            jax.ShapeDtypeStruct((group, rows, channels), BF16),
        ],
        input_output_aliases={4 + i: i for i in range(len(held))},
        scratch_shapes=[pltpu.VMEM((rows, channels), F32)],
        compiler_params=PARAMS,
        name="forward",
    )(x, og, kernel, weight, *held)


def chunk_of(t, sections, groups, ids):
    at = t - (sections - 1) + ids[0]
    inside = jnp.clip(at, 0, groups - 1)
    return inside, at == inside


def choose(which, refs, *at):
    value = refs[0][at]
    for i in range(1, len(refs)):
        value = jnp.where(which == i, refs[i][at], value)
    return value


def turn_kernel(t, sections, height, width, count, n_recv, n_next, ids, og_ref, raw_ref, gain_ref, pre_ref, x_ref, w_ref, kernel_ref, *rest):
    recvs, tots, nexts = rest[:n_recv], rest[n_recv : 2 * n_recv], rest[2 * n_recv : 2 * n_recv + n_next]
    u_out, part_out, total_out, pg_out, dg_out, rows_s, dg_s = rest[2 * n_recv + n_next :]
    group, rows, channels = u_out.shape
    groups = x_ref.shape[0] // group
    place, valid = chunk_of(t, sections, groups, ids)
    top = ids[0] == sections - 1
    side = ids[0] % 2 if n_recv > 1 else 0
    inverse = 1.0 / count

    def upstream(g, line, lanes):
        own = og_ref[place * group + g, line, lanes]
        return (jnp.where(top, own, choose(side, recvs, g, line, lanes)) if n_recv else own).astype(F32)

    def one(g, carry):
        slot = place * group + g

        def reduced(row):
            own = raw_ref[slot, 2 + row : 3 + row, :]
            return jnp.where(top, own, choose(side, tots, g, slice(row, row + 1), slice(None))) if n_recv else own

        center = raw_ref[slot, 0:1, :] * inverse
        square = raw_ref[slot, 1:2, :] * inverse
        inv = lax.rsqrt(square - center * center + epsilon)
        sum_grad = reduced(0)
        sum_cross = inv * (reduced(1) - center * sum_grad)
        total_out[g, 0:1, :] = sum_cross
        total_out[g, 1:2, :] = sum_grad
        scale = gain_ref[...] * inv
        slope = -scale * inv * sum_cross * inverse
        rows_s[0:1, :] = scale
        rows_s[1:2, :] = slope
        rows_s[2:3, :] = -scale * sum_grad * inverse - slope * center

        def grads(lanes):
            u = upstream(g, slice(None), lanes)
            pre = pre_ref[slot, :, lanes].astype(F32)
            pg_out[g, :, lanes] = (rows_s[0:1, lanes] * u + rows_s[1:2, lanes] * pre + rows_s[2:3, lanes]).astype(BF16)

        lane_loop(channels, grads)
        dg_s[...] = lax.dot_general(
            pg_out[g], w_ref[...], (((1,), (1,)), ((), ())), preferred_element_type=F32
        )

        def conv(lanes):
            taps = kernel_rows(kernel_ref, lanes)

            def parts(h):
                v = dg_s[h * width : (h + 1) * width, lanes]
                dg_out[g, h * width : (h + 1) * width, lanes] = v.astype(BF16)
                cols = cyclic(v, width)
                return [sum(taps[i][2 - j] * cols[j] for j in range(3)) for i in range(3)]

            window = [None, parts(0), None]
            first = second = None
            for h in range(height):
                window[2] = parts(h + 1) if h + 1 < height else None
                total = window[1][1]
                if window[0] is not None:
                    total = total + window[0][2]
                if window[2] is not None:
                    total = total + window[2][0]
                window = [window[1], window[2], None]
                line = slice(h * width, (h + 1) * width)
                x = x_ref[slot, line, lanes].astype(F32)
                fresh = (upstream(g, line, lanes) + jnp.where(x > 0.0, total, 0.0)).astype(BF16)
                u_out[g, line, lanes] = fresh
                if n_next:
                    fresh = fresh.astype(F32)
                    mixed = fresh * choose(place, nexts, g, line, lanes).astype(F32)
                    first = fresh if first is None else first + fresh
                    second = mixed if second is None else second + mixed
            if n_next:
                part_out[g, 0:1, lanes] = col_sum(first)
                part_out[g, 1:2, lanes] = col_sum(second)

        lane_loop(channels, conv)
        return carry

    @pl.when(valid)
    def _():
        lax.fori_loop(0, group, one, 0)


def turn(t, sections, ids, og, raw, gain, pre, x, weight, kernel, recvs, tots, nexts, height, width, count, group):
    micros, rows, channels = x.shape
    sent = jax.ShapeDtypeStruct((group, rows, channels), BF16)
    pair = jax.ShapeDtypeStruct((group, 2, channels), F32)
    return pl.pallas_call(
        functools.partial(turn_kernel, t, sections, height, width, count, len(recvs), len(nexts)),
        in_specs=[SMEM] + [VMEM] * (7 + 2 * len(recvs) + len(nexts)),
        out_specs=[VMEM] * 5,
        scratch_shapes=[
            pltpu.VMEM((8, channels), F32),
            pltpu.VMEM((rows, channels), F32),
        ],
        out_shape=[sent, pair, pair, sent, sent],
        compiler_params=PARAMS,
        name="turn",
    )(ids, og, raw, gain, pre, x, weight, kernel, *recvs, *tots, *nexts)


def cross_kernel(u_ref, next_ref, out):
    group, rows, channels = u_ref.shape
    for g in range(group):

        def sums(lanes):
            u = u_ref[g, :, lanes].astype(F32)
            out[g, 0:1, lanes] = col_sum(u)
            out[g, 1:2, lanes] = col_sum(u * next_ref[g, :, lanes].astype(F32))

        lane_loop(channels, sums)


def cross(u, following):
    group, rows, channels = u.shape
    return pl.pallas_call(
        cross_kernel,
        in_specs=[VMEM, VMEM],
        out_specs=VMEM,
        out_shape=jax.ShapeDtypeStruct((group, 2, channels), F32),
        compiler_params=PARAMS,
        name="cross",
    )(u, following)


def terms_kernel(t, sections, height, width, first, last, ids, x_ref, depth_ref, u_ref, pg_ref, dg_ref, total_ref, *rest):
    if not first:
        acc_ref, sums_ref, weight_ref = rest[:3]
        rest = rest[4:]
    else:
        acc_ref = sums_ref = weight_ref = None
    if last:
        acc_s, weight_out, sem = rest[-3:]
        table_out, sums_out, act_out, keep_out, send_out = rest[:-3]
        acc_out = acc_s
    else:
        acc_out, sums_out, weight_out, act_out, sem = rest
    group, rows, channels = u_ref.shape
    groups = x_ref.shape[0] // group
    place, valid = chunk_of(t, sections, groups, ids)

    def moves():
        return pltpu.make_async_copy(u_ref, act_out.at[pl.ds(place * group, group)], sem)

    @pl.when(valid)
    def _():
        moves().start()

    acc_out[...] = jnp.zeros_like(acc_out) if first else acc_ref[...]
    extra = total_ref[0]
    for g in range(1, group):
        extra = extra + total_ref[g]
    extra = jnp.where(valid, extra, 0.0)
    sums_out[...] = extra if first else sums_ref[...] + extra

    def one(g, carry):
        slot = place * group + g

        def terms(lanes):
            acc = [[None] * 3 for _ in range(3)]
            grads = [None] + [dg_ref[g, h * width : (h + 1) * width, lanes].astype(F32) for h in range(height)] + [None]
            for h in range(height):
                v = jnp.maximum(x_ref[slot, h * width : (h + 1) * width, lanes].astype(F32), 0.0)
                cols = cyclic(v, width)
                for i in range(3):
                    up = grads[h + 2 - i]
                    if up is None:
                        continue
                    for j in range(3):
                        p = cols[j] * up
                        acc[i][j] = p if acc[i][j] is None else acc[i][j] + p
            for i in range(3):
                for j in range(3):
                    row = slice(3 * i + j, 3 * i + j + 1)
                    acc_out[row, lanes] += col_sum(acc[i][j])

        lane_loop(channels, terms)
        return carry

    @pl.when(valid)
    def _():
        lax.fori_loop(0, group, one, 0)
        at = pl.ds(place * group, group)
        fresh = lax.dot_general(
            depth_ref[at].reshape(group * rows, channels),
            pg_ref[...].reshape(group * rows, channels),
            (((0,), (0,)), ((), ())),
            preferred_element_type=F32,
        )
        weight_out[...] = fresh if first else weight_ref[...] + fresh

    if first or last:

        @pl.when(jnp.logical_not(valid))
        def _():
            weight_out[...] = jnp.zeros_like(weight_out) if first else weight_ref[...]

    if last:
        half = channels // 2
        core = ids[1] % 2
        keep_out[...] = weight_out[pl.ds(pl.multiple_of(core * half, half), half), :]
        other = pl.multiple_of((1 - core) * half, half)
        send_out[0:half, :] = weight_out[pl.ds(other, half), :].astype(BF16)
        send_out[half : half + 16, :] = acc_out[...].astype(BF16)
        table_out[...] = acc_out[...]

    @pl.when(valid)
    def _():
        moves().wait()


def terms(t, sections, last, ids, x, depth, u, pg, dg, total, carried, height, width):
    micros, rows, channels = x.shape
    half = channels // 2
    table = jax.ShapeDtypeStruct((16, channels), F32)
    sums = jax.ShapeDtypeStruct((2, channels), F32)
    square = jax.ShapeDtypeStruct((channels, channels), F32)
    act = jax.ShapeDtypeStruct(x.shape, BF16)
    n = 7
    first = not carried
    scratch = [pltpu.SemaphoreType.DMA]
    if last:
        out_shape = [
            table,
            sums,
            act,
            jax.ShapeDtypeStruct((half, channels), F32),
            jax.ShapeDtypeStruct((half + 16, channels), BF16),
        ]
        out_specs = [VMEM, VMEM, ANY, VMEM, VMEM]
        scratch = [pltpu.VMEM((16, channels), F32), pltpu.VMEM((channels, channels), F32)] + scratch
        aliases = {} if first else {n + 3: 2}
    else:
        out_shape = [table, sums, square, act]
        out_specs = [VMEM, VMEM, VMEM, ANY]
        aliases = {} if first else {n + 2: 2, n + 3: 3}
    return pl.pallas_call(
        functools.partial(terms_kernel, t, sections, height, width, first, last),
        in_specs=[SMEM] + [VMEM] * 6 + ([] if first else [VMEM] * 3 + [ANY]),
        out_specs=out_specs,
        out_shape=out_shape,
        scratch_shapes=scratch,
        input_output_aliases=aliases,
        compiler_params=PARAMS,
        name="terms",
    )(ids, x, depth, u, pg, dg, total, *carried)


def split_kernel(chips, chunk, where_ref, keep_ref, sent_ref, recv_ref, own_out, *outs):
    half = chips * chunk
    chip = where_ref[1] // 2
    table = sent_ref[half : half + 16, :].astype(F32) + recv_ref[half : half + 16, :].astype(F32)
    for k in range(chips):
        at = pl.multiple_of((chip ^ k) * chunk, chunk)
        piece = keep_ref[pl.ds(at, chunk), :] + recv_ref[pl.ds(at, chunk), :].astype(F32)
        if k == 0:
            own_out[0:chunk, :] = piece
            own_out[chunk : chunk + 16, :] = table.astype(BF16).astype(F32)
        else:
            outs[k - 1][0:chunk, :] = piece.astype(BF16)
            outs[k - 1][chunk : chunk + 16, :] = table.astype(BF16)


def split(where, keep, sent, recv, chips):
    half, channels = keep.shape
    chunk = half // chips
    vmem = pl.BlockSpec(memory_space=pltpu.VMEM)
    return pl.pallas_call(
        functools.partial(split_kernel, chips, chunk),
        in_specs=[pl.BlockSpec(memory_space=pltpu.SMEM), vmem, vmem, vmem],
        out_specs=[vmem] * chips,
        out_shape=[jax.ShapeDtypeStruct((chunk + 16, channels), F32)]
        + [jax.ShapeDtypeStruct((chunk + 16, channels), BF16)] * (chips - 1),
        compiler_params=PARAMS,
        name="split",
    )(where, keep, sent, recv)


def merge_kernel(chunk, own_ref, *refs):
    parts = [own_ref[...]] + [r[...].astype(F32) for r in refs[:-2]]
    while len(parts) > 1:
        parts = [a + b for a, b in zip(parts[::2], parts[1::2])]
    refs[-2][...] = parts[0][0:chunk, :].astype(BF16)
    refs[-1][...] = parts[0][chunk:, :]


def merge(own, recvs):
    chunk, channels = own.shape[0] - 16, own.shape[1]
    vmem = pl.BlockSpec(memory_space=pltpu.VMEM)
    return pl.pallas_call(
        functools.partial(merge_kernel, chunk),
        in_specs=[vmem] * (1 + len(recvs)),
        out_specs=[vmem] * 2,
        out_shape=[
            jax.ShapeDtypeStruct((chunk, channels), BF16),
            jax.ShapeDtypeStruct((16, channels), F32),
        ],
        compiler_params=PARAMS,
        name="merge",
    )(own, *recvs)


def gather_kernel(chunk, where_ref, *refs):
    for k, ref in enumerate(refs[:-1]):
        at = pl.multiple_of((where_ref[1] // 2 ^ k) * chunk, chunk)
        refs[-1][pl.ds(at, chunk), :] = ref[...]


def gather(where, parts):
    chunk, channels = parts[0].shape
    vmem = pl.BlockSpec(memory_space=pltpu.VMEM)
    return pl.pallas_call(
        functools.partial(gather_kernel, chunk),
        in_specs=[pl.BlockSpec(memory_space=pltpu.SMEM)] + [vmem] * len(parts),
        out_specs=vmem,
        out_shape=jax.ShapeDtypeStruct((chunk * len(parts), channels), BF16),
        compiler_params=PARAMS,
        name="gather",
    )(where, *parts)


def widen_kernel(half, where_ref, own_ref, recv_ref, out_ref):
    core = where_ref[1] % 2
    out_ref[0, pl.ds(pl.multiple_of(core * half, half), half), :] = own_ref[...].astype(F32)
    out_ref[0, pl.ds(pl.multiple_of((1 - core) * half, half), half), :] = recv_ref[...].astype(F32)


def widen(where, own, recv):
    half, channels = own.shape
    vmem = pl.BlockSpec(memory_space=pltpu.VMEM)
    return pl.pallas_call(
        functools.partial(widen_kernel, half),
        in_specs=[pl.BlockSpec(memory_space=pltpu.SMEM), vmem, vmem],
        out_specs=vmem,
        out_shape=jax.ShapeDtypeStruct((1, 2 * half, channels), F32),
        compiler_params=PARAMS,
        name="widen",
    )(where, own, recv)


def tree(parts):
    while len(parts) > 1:
        parts = [a + b for a, b in zip(parts[::2], parts[1::2])]
    return parts[0]


def body(acts, out_grad, depth_kernel, point_weight, bn_gain):
    sections = lax.axis_size("section")
    replicas = lax.axis_size("dp")
    micros, images, height, width, channels = acts.shape[1:]
    rows = images * height * width
    count = rows * replicas
    chips = replicas // 2
    group = GROUP if micros % GROUP == 0 else 1
    groups = micros // group
    turns = sections + groups - 1
    x = acts.reshape(micros, rows, channels)
    og = out_grad.reshape(micros, rows, channels)
    kernel = depth_kernel[0]
    weight = point_weight[0]
    gain = bn_gain
    ids = jnp.stack([lax.axis_index("section"), lax.axis_index("dp")]).astype(jnp.int32)

    def swap(v, k):
        return lax.ppermute(v, "dp", [(i, i ^ k) for i in range(replicas)])

    def at_work(t):
        return [s for s in range(1, sections) if 0 <= t - (sections - 1 - s) < groups]

    def trade(v):
        return lax.ppermute(v, "section", [(s, s ^ 1) for s in range(sections)])

    def down(v, t):
        if sections % 2 == 0 and all(s % 2 for s in at_work(t)):
            return [trade(v)]
        return [lax.ppermute(v, "section", [(s, (s - 1) % sections) for s in range(sections)])]

    def up(v, lowers):
        return lax.ppermute(v, "section", [(i, i + 1) for i in lowers])

    def everywhere(v):
        v = v + swap(v, 1)
        return tree([v] + [swap(v, k) for k in range(2, replicas, 2)])

    held = []
    copies = []
    x_far, og_far = (pltpu.with_memory_space_constraint(v, pltpu.HBM) for v in (x, og))
    for i in range(groups):
        *held, copy = forward(i, x_far, og_far, kernel, weight, held, height, width, group)
        copies.append(copy)
    depth, pre, raw = held
    soonest = trade(copies[0]) if sections % 2 == 0 else up(copies[0], [sections - 2])
    nexts = [up(copies[0], range(sections - 2))]
    raw = everywhere(raw)

    recvs, tots, collected = [], [], ()
    for t in range(turns):
        last = t + 1 == turns
        fresh, part, total, pg, dg = turn(
            t, sections, ids, og, raw, gain, pre, x, weight, kernel, recvs, tots,
            [] if last or t == 0 else nexts, height, width, count, group,
        )
        if not last:
            recvs = down(fresh, t)
            if t == 0:
                part = cross(fresh, soonest)
                later, part = lax.optimization_barrier((copies[1:], part))
                nexts += [up(v, range(sections - 1)) for v in later]
            tots = down(everywhere(part), t)
        collected = terms(t, sections, last, ids, x, depth, fresh, pg, dg, total, collected, height, width)
        if not last:
            gain, collected = lax.optimization_barrier((gain, collected))
    table, sums, act, keep, send = collected
    got = split(ids, keep, send, swap(send, 1), chips)
    chunk, table = merge(got[0], [swap(v, 2 * k) for k, v in enumerate(got[1:], 1)])
    half = gather(ids, [chunk] + [swap(chunk, 2 * k) for k in range(1, chips)])
    point = widen(ids, half, swap(half, 1))
    return (act.reshape(acts.shape), point, table[:9].reshape(1, 3, 3, channels), sums[0:1], sums[1:2])


def solution(mesh):
    return jax.shard_map(
        body,
        mesh=mesh,
        in_specs=(
            P("section", None, "dp", None, None, None),
            P(None, "dp", None, None, None),
            P("section", None, None, None),
            P("section", None, None),
            P("section", None),
        ),
        out_specs=(
            P("section", None, "dp", None, None, None),
            P("section", None, None),
            P("section", None, None, None),
            P("section", None),
            P("section", None),
        ),
        check_vma=False,
    )
```

```python
import functools

import jax
import jax.numpy as jnp
from jax import lax
from jax.experimental import pallas as pl
from jax.experimental.pallas import tpu as pltpu
from jax.sharding import PartitionSpec as P

epsilon = 1e-05
LANES = 128
F32 = jnp.float32
BF16 = jnp.bfloat16

GROUP = 2
PARAMS = pltpu.CompilerParams(vmem_limit_bytes=16 << 20)


def cyclic(v, width):
    col = lax.broadcasted_iota(jnp.int32, v.shape, 0)
    before = jnp.where(col == 0, 0.0, pltpu.roll(v, 1, 0))
    after = jnp.where(col == width - 1, 0.0, pltpu.roll(v, width - 1, 0))
    return before, v, after


def lane_loop(channels, work):
    def step(i, carry):
        work(pl.ds(pl.multiple_of(i * LANES, LANES), LANES))
        return carry

    lax.fori_loop(0, channels // LANES, step, 0)


def kernel_rows(kernel_ref, lanes):
    return [[kernel_ref[i, j : j + 1, lanes].astype(F32) for j in range(3)] for i in range(3)]


def col_sum(v):
    return jnp.sum(v, axis=0, keepdims=True)


VMEM = pl.BlockSpec(memory_space=pltpu.VMEM)
SMEM = pl.BlockSpec(memory_space=pltpu.SMEM)
ANY = pl.BlockSpec(memory_space=pl.ANY)


def forward_group(part, height, width, x_ref, og_ref, kernel_ref, w_ref, depth_ref, pre_ref, raw_ref, copy_ref, pre_s, ready):
    channels = x_ref.shape[-1]
    group = copy_ref.shape[0]

    def one(g, carry):
        slot = part * group + g
        ready(0, slot)

        def conv(lanes):
            taps = kernel_rows(kernel_ref, lanes)

            def parts(h):
                v = jnp.maximum(x_ref[slot, h * width : (h + 1) * width, lanes].astype(F32), 0.0)
                cols = cyclic(v, width)
                return [sum(taps[i][j] * cols[j] for j in range(3)) for i in range(3)]

            window = [None, parts(0), None]
            for h in range(height):
                window[2] = parts(h + 1) if h + 1 < height else None
                total = window[1][1]
                if window[0] is not None:
                    total = total + window[0][0]
                if window[2] is not None:
                    total = total + window[2][2]
                depth_ref[slot, h * width : (h + 1) * width, lanes] = total.astype(BF16)
                window = [window[1], window[2], None]

        lane_loop(channels, conv)
        ready(1, slot)
        pre_s[...] = jnp.dot(depth_ref[slot], w_ref[...], preferred_element_type=F32)
        ready(2, slot)

        def sums(lanes):
            p = pre_s[:, lanes]
            v = og_ref[slot, :, lanes].astype(F32)
            short = p.astype(BF16)
            pre_ref[slot, :, lanes] = short
            copy_ref[g, :, lanes] = short
            for row, value in enumerate((p, p * p, v, v * p)):
                raw_ref[slot, row : row + 1, lanes] = col_sum(value)

        lane_loop(channels, sums)
        return carry

    lax.fori_loop(0, group, one, 0)


def load_kernel(height, width, ids, x_far, og_far, kernel_far, w_far, gain_far, *rest):
    depth_ref, pre_ref, raw_ref, copy_ref, x_ref, og_ref, kernel_ref, w_ref, gain_ref, pre_s, few, many = rest
    micros = x_ref.shape[0]
    group = copy_ref.shape[0]
    weights = pltpu.make_async_copy(w_far, w_ref, few.at[0])
    table = pltpu.make_async_copy(kernel_far, kernel_ref, few.at[1])
    gains = pltpu.make_async_copy(gain_far, gain_ref, few.at[2])

    def inputs(m):
        return pltpu.make_async_copy(x_far.at[m], x_ref.at[m], many.at[0, m])

    def outputs(m):
        return pltpu.make_async_copy(og_far.at[m], og_ref.at[m], many.at[1, m])

    table.start()
    inputs(0).start()
    weights.start()
    outputs(0).start()
    for m in range(1, micros):
        inputs(m).start()
        outputs(m).start()
    gains.start()

    def ready(stage, slot):
        if stage == 0:
            inputs(slot).wait()

            @pl.when(slot == 0)
            def _():
                table.wait()

        elif stage == 1:

            @pl.when(slot == 0)
            def _():
                weights.wait()

        else:
            outputs(slot).wait()

    forward_group(0, height, width, x_ref, og_ref, kernel_ref, w_ref, depth_ref, pre_ref, raw_ref, copy_ref, pre_s, ready)
    for m in range(group, micros):
        inputs(m).wait()
        outputs(m).wait()
    gains.wait()


def load(ids, x, og, kernel, weight, gain, height, width, group):
    micros, rows, channels = x.shape
    table = jax.ShapeDtypeStruct((micros, 4, channels), F32)
    args = [pltpu.with_memory_space_constraint(v, pltpu.HBM) for v in (x, og, kernel, weight, gain)]
    return pl.pallas_call(
        functools.partial(load_kernel, height, width),
        in_specs=[SMEM] + [ANY] * 5,
        out_specs=[VMEM] * 9,
        out_shape=[
            jax.ShapeDtypeStruct(x.shape, BF16),
            jax.ShapeDtypeStruct(x.shape, BF16),
            table,
            jax.ShapeDtypeStruct((group, rows, channels), BF16),
        ]
        + [jax.ShapeDtypeStruct(v.shape, v.dtype) for v in (x, og, kernel, weight, gain)],
        scratch_shapes=[
            pltpu.VMEM((rows, channels), F32),
            pltpu.SemaphoreType.DMA((3,)),
            pltpu.SemaphoreType.DMA((2, micros)),
        ],
        compiler_params=PARAMS,
        name="load",
    )(ids, *args)


def forward_kernel(part, height, width, x_ref, og_ref, kernel_ref, w_ref, *rest):
    outs = rest[3:]
    group = outs[3].shape[0]
    for old, new in zip(rest[:3], outs):
        new[0 : part * group] = old[0 : part * group]
    forward_group(part, height, width, x_ref, og_ref, kernel_ref, w_ref, *outs, lambda stage, slot: None)


def forward(part, x, og, kernel, weight, held, height, width, group):
    micros, rows, channels = x.shape
    return pl.pallas_call(
        functools.partial(forward_kernel, part, height, width),
        in_specs=[VMEM] * 7,
        out_specs=[VMEM] * 4,
        out_shape=[jax.ShapeDtypeStruct(v.shape, v.dtype) for v in held]
        + [jax.ShapeDtypeStruct((group, rows, channels), BF16)],
        input_output_aliases={4 + i: i for i in range(3)},
        scratch_shapes=[pltpu.VMEM((rows, channels), F32)],
        compiler_params=PARAMS,
        name="forward",
    )(x, og, kernel, weight, *held)


def add_kernel(a_ref, b_ref, out_ref):
    out_ref[...] = a_ref[...] + b_ref[...]


def add(a, b):
    return pl.pallas_call(
        add_kernel,
        in_specs=[VMEM, VMEM],
        out_specs=VMEM,
        out_shape=jax.ShapeDtypeStruct(a.shape, a.dtype),
        compiler_params=PARAMS,
        name="add",
    )(a, b)


def chunk_of(t, sections, groups, ids):
    at = t - (sections - 1) + ids[0]
    inside = jnp.clip(at, 0, groups - 1)
    return inside, at == inside


def choose(which, refs, *at):
    value = refs[0][at]
    for i in range(1, len(refs)):
        value = jnp.where(which == i, refs[i][at], value)
    return value


def turn_kernel(t, sections, last, height, width, count, n_recv, n_next, n_raw, n_own, ids, gain_ref, pre_ref, x_ref, w_ref, kernel_ref, *rest):
    raws, rest = rest[:n_raw], rest[n_raw:]
    owns, rest = rest[:n_own], rest[n_own:]
    recvs, tots, nexts = rest[:n_recv], rest[n_recv : 2 * n_recv], rest[2 * n_recv : 2 * n_recv + n_next]
    outs = rest[2 * n_recv + n_next :]
    if last:
        total_out, pg_out, dg_out, rows_s, dg_s = outs
    else:
        u_out, part_out, total_out, pg_out, dg_out, rows_s, dg_s = outs
    group, rows, channels = pg_out.shape
    groups = x_ref.shape[0] // group
    place, valid = chunk_of(t, sections, groups, ids)
    top = ids[0] == sections - 1
    side = ids[0] % 2 if n_recv > 1 else 0
    inverse = 1.0 / count

    def upstream(g, line, lanes):
        value = choose(side, recvs, g, line, lanes) if n_recv else None
        if n_own:
            own = owns[0][place * group + g, line, lanes]
            value = jnp.where(top, own, value) if n_recv else own
        return value.astype(F32)

    def one(g, carry):
        slot = place * group + g

        def raw(row):
            return tree([r[slot, row : row + 1, :] for r in raws])

        def reduced(row):
            value = choose(side, tots, g, slice(row, row + 1), slice(None)) if n_recv else None
            if n_own:
                value = jnp.where(top, raw(2 + row), value) if n_recv else raw(2 + row)
            return value

        center = raw(0) * inverse
        square = raw(1) * inverse
        inv = lax.rsqrt(square - center * center + epsilon)
        sum_grad = reduced(0)
        sum_cross = inv * (reduced(1) - center * sum_grad)
        total_out[g, 0:1, :] = sum_cross
        total_out[g, 1:2, :] = sum_grad
        scale = gain_ref[...] * inv
        slope = -scale * inv * sum_cross * inverse
        rows_s[0:1, :] = scale
        rows_s[1:2, :] = slope
        rows_s[2:3, :] = -scale * sum_grad * inverse - slope * center

        def grads(lanes):
            u = upstream(g, slice(None), lanes)
            pre = pre_ref[slot, :, lanes].astype(F32)
            pg_out[g, :, lanes] = (rows_s[0:1, lanes] * u + rows_s[1:2, lanes] * pre + rows_s[2:3, lanes]).astype(BF16)

        lane_loop(channels, grads)
        dg_s[...] = lax.dot_general(
            pg_out[g], w_ref[...], (((1,), (1,)), ((), ())), preferred_element_type=F32
        )

        if last:
            dg_out[g] = dg_s[...].astype(BF16)
            return carry

        def conv(lanes):
            taps = kernel_rows(kernel_ref, lanes)

            def parts(h):
                v = dg_s[h * width : (h + 1) * width, lanes]
                dg_out[g, h * width : (h + 1) * width, lanes] = v.astype(BF16)
                cols = cyclic(v, width)
                return [sum(taps[i][2 - j] * cols[j] for j in range(3)) for i in range(3)]

            window = [None, parts(0), None]
            first = second = None
            for h in range(height):
                window[2] = parts(h + 1) if h + 1 < height else None
                total = window[1][1]
                if window[0] is not None:
                    total = total + window[0][2]
                if window[2] is not None:
                    total = total + window[2][0]
                window = [window[1], window[2], None]
                line = slice(h * width, (h + 1) * width)
                x = x_ref[slot, line, lanes].astype(F32)
                fresh = (upstream(g, line, lanes) + jnp.where(x > 0.0, total, 0.0)).astype(BF16)
                u_out[g, line, lanes] = fresh
                if n_next:
                    fresh = fresh.astype(F32)
                    mixed = fresh * choose(place, nexts, g, line, lanes).astype(F32)
                    first = fresh if first is None else first + fresh
                    second = mixed if second is None else second + mixed
            if n_next:
                part_out[g, 0:1, lanes] = col_sum(first)
                part_out[g, 1:2, lanes] = col_sum(second)

        lane_loop(channels, conv)
        return carry

    @pl.when(valid)
    def _():
        lax.fori_loop(0, group, one, 0)


def turn(t, sections, last, ids, og, raws, gain, pre, x, weight, kernel, recvs, tots, nexts, height, width, count, group):
    micros, rows, channels = x.shape
    owns = [og] if t < micros // group or not recvs else []
    sent = jax.ShapeDtypeStruct((group, rows, channels), BF16)
    pair = jax.ShapeDtypeStruct((group, 2, channels), F32)
    return pl.pallas_call(
        functools.partial(
            turn_kernel, t, sections, last, height, width, count,
            len(recvs), len(nexts), len(raws), len(owns),
        ),
        in_specs=[SMEM] + [VMEM] * (5 + len(raws) + len(owns) + 2 * len(recvs) + len(nexts)),
        out_specs=[VMEM] * (3 if last else 5),
        scratch_shapes=[
            pltpu.VMEM((8, channels), F32),
            pltpu.VMEM((rows, channels), F32),
        ],
        out_shape=([] if last else [sent, pair]) + [pair, sent, sent],
        compiler_params=PARAMS,
        name="turn",
    )(ids, gain, pre, x, weight, kernel, *raws, *owns, *recvs, *tots, *nexts)


def cross_kernel(u_ref, next_ref, out):
    group, rows, channels = u_ref.shape
    for g in range(group):

        def sums(lanes):
            u = u_ref[g, :, lanes].astype(F32)
            out[g, 0:1, lanes] = col_sum(u)
            out[g, 1:2, lanes] = col_sum(u * next_ref[g, :, lanes].astype(F32))

        lane_loop(channels, sums)


def cross(u, following):
    group, rows, channels = u.shape
    return pl.pallas_call(
        cross_kernel,
        in_specs=[VMEM, VMEM],
        out_specs=VMEM,
        out_shape=jax.ShapeDtypeStruct((group, 2, channels), F32),
        compiler_params=PARAMS,
        name="cross",
    )(u, following)


def terms_kernel(t, sections, height, width, first, last, ids, x_ref, depth_ref, pg_ref, dg_ref, total_ref, *rest):
    if not last:
        u_ref, rest = rest[0], rest[1:]
    if not first:
        acc_ref, sums_ref, weight_ref = rest[:3]
        rest = rest[3:] if last else rest[4:]
    else:
        acc_ref = sums_ref = weight_ref = None
    if last:
        table_out, sums_out, bias_out, keep_out, send_out, acc_out, weight_out = rest
    else:
        acc_out, sums_out, weight_out, act_out, sem = rest
    group, rows, channels = pg_ref.shape
    groups = x_ref.shape[0] // group
    place, valid = chunk_of(t, sections, groups, ids)
    if not last:

        def moves():
            return pltpu.make_async_copy(u_ref, act_out.at[pl.ds(place * group, group)], sem)

        @pl.when(valid)
        def _():
            moves().start()

    acc_out[...] = jnp.zeros_like(acc_out) if first else acc_ref[...]
    extra = total_ref[0]
    for g in range(1, group):
        extra = extra + total_ref[g]
    extra = jnp.where(valid, extra, 0.0)
    extra = extra if first else sums_ref[...] + extra
    if last:
        sums_out[...] = extra[0:1]
        bias_out[...] = extra[1:2]
    else:
        sums_out[...] = extra

    def one(g, carry):
        slot = place * group + g

        def terms(lanes):
            acc = [[None] * 3 for _ in range(3)]
            grads = [None] + [dg_ref[g, h * width : (h + 1) * width, lanes].astype(F32) for h in range(height)] + [None]
            for h in range(height):
                v = jnp.maximum(x_ref[slot, h * width : (h + 1) * width, lanes].astype(F32), 0.0)
                cols = cyclic(v, width)
                for i in range(3):
                    up = grads[h + 2 - i]
                    if up is None:
                        continue
                    for j in range(3):
                        p = cols[j] * up
                        acc[i][j] = p if acc[i][j] is None else acc[i][j] + p
            for i in range(3):
                for j in range(3):
                    row = slice(3 * i + j, 3 * i + j + 1)
                    acc_out[row, lanes] += col_sum(acc[i][j])

        lane_loop(channels, terms)
        return carry

    @pl.when(valid)
    def _():
        lax.fori_loop(0, group, one, 0)
        at = pl.ds(place * group, group)
        fresh = lax.dot_general(
            depth_ref[at].reshape(group * rows, channels),
            pg_ref[...].reshape(group * rows, channels),
            (((0,), (0,)), ((), ())),
            preferred_element_type=F32,
        )
        weight_out[...] = fresh if first else weight_ref[...] + fresh

    @pl.when(jnp.logical_not(valid))
    def _():
        weight_out[...] = jnp.zeros_like(weight_out) if first else weight_ref[...]

    if last:
        half = channels // 2
        core = ids[1] % 2
        keep_out[...] = weight_out[pl.ds(pl.multiple_of(core * half, half), half), :]
        other = pl.multiple_of((1 - core) * half, half)
        send_out[0:half, :] = weight_out[pl.ds(other, half), :].astype(BF16)
        send_out[half : half + 16, :] = acc_out[...].astype(BF16)
        table_out[...] = acc_out[...]
    else:

        @pl.when(valid)
        def _():
            moves().wait()


def terms(t, sections, last, ids, x, depth, u, pg, dg, total, carried, height, width):
    micros, rows, channels = x.shape
    half = channels // 2
    table = jax.ShapeDtypeStruct((16, channels), F32)
    sums = jax.ShapeDtypeStruct((2, channels), F32)
    square = jax.ShapeDtypeStruct((channels, channels), F32)
    act = jax.ShapeDtypeStruct(x.shape, BF16)
    first = not carried
    if last:
        carried = carried[:3]
        out_shape = [
            table,
            jax.ShapeDtypeStruct((1, channels), F32),
            jax.ShapeDtypeStruct((1, channels), F32),
            jax.ShapeDtypeStruct((half, channels), F32),
            jax.ShapeDtypeStruct((half + 16, channels), BF16),
        ]
        in_specs = [VMEM] * len(carried)
        out_specs = [VMEM] * 5
        scratch = [pltpu.VMEM((16, channels), F32), pltpu.VMEM((channels, channels), F32)]
        aliases = {}
    else:
        out_shape = [table, sums, square, act]
        in_specs = [VMEM] + ([] if first else [VMEM] * 3 + [ANY])
        out_specs = [VMEM, VMEM, VMEM, ANY]
        scratch = [pltpu.SemaphoreType.DMA]
        aliases = {} if first else {9: 2, 10: 3}
        carried = (u, *carried)
    return pl.pallas_call(
        functools.partial(terms_kernel, t, sections, height, width, first, last),
        in_specs=[SMEM] + [VMEM] * 5 + in_specs,
        out_specs=out_specs,
        out_shape=out_shape,
        scratch_shapes=scratch,
        input_output_aliases=aliases,
        compiler_params=PARAMS,
        name="terms",
    )(ids, x, depth, pg, dg, total, *carried)


def finish_kernel(t, sections, height, width, n_recv, n_own, ids, x_ref, dg_ref, kernel_ref, *rest):
    owns, rest = rest[:n_own], rest[n_own:]
    recvs = rest[:n_recv]
    act_out, u_s, sem = rest[-3:]
    group, rows, channels = dg_ref.shape
    groups = x_ref.shape[0] // group
    place, valid = chunk_of(t, sections, groups, ids)
    top = ids[0] == sections - 1

    def one(g, carry):
        slot = place * group + g

        def conv(lanes):
            taps = kernel_rows(kernel_ref, lanes)

            def parts(h):
                cols = cyclic(dg_ref[g, h * width : (h + 1) * width, lanes].astype(F32), width)
                return [sum(taps[i][2 - j] * cols[j] for j in range(3)) for i in range(3)]

            window = [None, parts(0), None]
            for h in range(height):
                window[2] = parts(h + 1) if h + 1 < height else None
                total = window[1][1]
                if window[0] is not None:
                    total = total + window[0][2]
                if window[2] is not None:
                    total = total + window[2][0]
                window = [window[1], window[2], None]
                line = slice(h * width, (h + 1) * width)
                u = recvs[0][g, line, lanes] if n_recv else None
                if n_own:
                    own = owns[0][slot, line, lanes]
                    u = jnp.where(top, own, u) if n_recv else own
                x = x_ref[slot, line, lanes].astype(F32)
                u_s[g, line, lanes] = (u.astype(F32) + jnp.where(x > 0.0, total, 0.0)).astype(BF16)

        lane_loop(channels, conv)
        return carry

    @pl.when(valid)
    def _():
        lax.fori_loop(0, group, one, 0)
        move = pltpu.make_async_copy(u_s, act_out.at[pl.ds(place * group, group)], sem)
        move.start()
        move.wait()


def finish(t, sections, ids, og, x, dg, kernel, recvs, act, height, width):
    owns = [og] if t < x.shape[0] // dg.shape[0] or not recvs else []
    return pl.pallas_call(
        functools.partial(finish_kernel, t, sections, height, width, len(recvs), len(owns)),
        in_specs=[SMEM] + [VMEM] * (3 + len(owns) + len(recvs)) + [ANY] * len(act),
        out_specs=ANY,
        out_shape=jax.ShapeDtypeStruct(x.shape, BF16),
        scratch_shapes=[pltpu.VMEM(dg.shape, BF16), pltpu.SemaphoreType.DMA],
        input_output_aliases={4 + len(owns) + len(recvs): 0} if act else {},
        compiler_params=PARAMS,
        name="finish",
    )(ids, x, dg, kernel, *owns, *recvs, *act)


def split_kernel(chips, chunk, where_ref, keep_ref, sent_ref, recv_ref, own_out, *outs):
    half = chips * chunk
    chip = where_ref[1] // 2
    table = sent_ref[half : half + 16, :].astype(F32) + recv_ref[half : half + 16, :].astype(F32)
    for k in range(chips):
        at = pl.multiple_of((chip ^ k) * chunk, chunk)
        piece = keep_ref[pl.ds(at, chunk), :] + recv_ref[pl.ds(at, chunk), :].astype(F32)
        if k == 0:
            own_out[0:chunk, :] = piece
            own_out[chunk : chunk + 16, :] = table.astype(BF16).astype(F32)
        else:
            outs[k - 1][0:chunk, :] = piece.astype(BF16)
            outs[k - 1][chunk : chunk + 16, :] = table.astype(BF16)


def split(where, keep, sent, recv, chips):
    half, channels = keep.shape
    chunk = half // chips
    vmem = pl.BlockSpec(memory_space=pltpu.VMEM)
    return pl.pallas_call(
        functools.partial(split_kernel, chips, chunk),
        in_specs=[pl.BlockSpec(memory_space=pltpu.SMEM), vmem, vmem, vmem],
        out_specs=[vmem] * chips,
        out_shape=[jax.ShapeDtypeStruct((chunk + 16, channels), F32)]
        + [jax.ShapeDtypeStruct((chunk + 16, channels), BF16)] * (chips - 1),
        compiler_params=PARAMS,
        name="split",
    )(where, keep, sent, recv)


def merge_kernel(chunk, own_ref, *refs):
    parts = [own_ref[...]] + [r[...].astype(F32) for r in refs[:-2]]
    while len(parts) > 1:
        parts = [a + b for a, b in zip(parts[::2], parts[1::2])]
    refs[-2][...] = parts[0][0:chunk, :].astype(BF16)
    refs[-1][...] = parts[0][chunk:, :]


def merge(own, recvs):
    chunk, channels = own.shape[0] - 16, own.shape[1]
    vmem = pl.BlockSpec(memory_space=pltpu.VMEM)
    return pl.pallas_call(
        functools.partial(merge_kernel, chunk),
        in_specs=[vmem] * (1 + len(recvs)),
        out_specs=[vmem] * 2,
        out_shape=[
            jax.ShapeDtypeStruct((chunk, channels), BF16),
            jax.ShapeDtypeStruct((16, channels), F32),
        ],
        compiler_params=PARAMS,
        name="merge",
    )(own, *recvs)


def gather_kernel(chunk, where_ref, *refs):
    half_out, out_ref = refs[-2:]
    half = half_out.shape[0]
    start = (where_ref[1] % 2) * half
    for k, ref in enumerate(refs[:-2]):
        at = (where_ref[1] // 2 ^ k) * chunk
        value = ref[...]
        half_out[pl.ds(pl.multiple_of(at, chunk), chunk), :] = value
        out_ref[pl.ds(pl.multiple_of(start + at, chunk), chunk), :] = value.astype(F32)


def gather(where, parts):
    chunk, channels = parts[0].shape
    half = chunk * len(parts)
    return pl.pallas_call(
        functools.partial(gather_kernel, chunk),
        in_specs=[SMEM] + [VMEM] * len(parts),
        out_specs=[VMEM, VMEM],
        out_shape=[
            jax.ShapeDtypeStruct((half, channels), BF16),
            jax.ShapeDtypeStruct((2 * half, channels), F32),
        ],
        compiler_params=PARAMS,
        name="gather",
    )(where, *parts)


def widen_kernel(where_ref, recv_ref, out_in, out_ref, wide, sem):
    half = recv_ref.shape[0]
    wide[...] = recv_ref[...].astype(F32)
    other = pl.multiple_of((1 - where_ref[1] % 2) * half, half)
    move = pltpu.make_async_copy(wide, out_ref.at[pl.ds(other, half)], sem)
    move.start()
    move.wait()


def widen(where, recv, out):
    return pl.pallas_call(
        widen_kernel,
        in_specs=[SMEM, VMEM, ANY],
        out_specs=ANY,
        out_shape=jax.ShapeDtypeStruct(out.shape, F32),
        scratch_shapes=[pltpu.VMEM(recv.shape, F32), pltpu.SemaphoreType.DMA],
        input_output_aliases={2: 0},
        compiler_params=PARAMS,
        name="widen",
    )(where, recv, out)


def tree(parts):
    while len(parts) > 1:
        parts = [a + b for a, b in zip(parts[::2], parts[1::2])]
    return parts[0]


def body(acts, out_grad, depth_kernel, point_weight, bn_gain):
    sections = lax.axis_size("section")
    replicas = lax.axis_size("dp")
    micros, images, height, width, channels = acts.shape[1:]
    rows = images * height * width
    count = rows * replicas
    chips = replicas // 2
    group = GROUP if micros % GROUP == 0 else 1
    groups = micros // group
    turns = sections + groups - 1
    x = acts.reshape(micros, rows, channels)
    og = out_grad.reshape(micros, rows, channels)
    kernel = depth_kernel[0]
    weight = point_weight[0]
    gain = bn_gain
    ids = jnp.stack([lax.axis_index("section"), lax.axis_index("dp")]).astype(jnp.int32)

    def swap(v, k):
        return lax.ppermute(v, "dp", [(i, i ^ k) for i in range(replicas)])

    def at_work(t):
        return [s for s in range(1, sections) if 0 <= t - (sections - 1 - s) < groups]

    def trade(v):
        return lax.ppermute(v, "section", [(s, s ^ 1) for s in range(sections)])

    def down(v, t):
        if sections % 2 == 0 and all(s % 2 for s in at_work(t)):
            return [trade(v)]
        return [lax.ppermute(v, "section", [(s, (s - 1) % sections) for s in range(sections)])]

    def up(v, wrap):
        pairs = [(s, (s + 1) % sections) for s in range(sections if wrap else sections - 1)]
        return lax.ppermute(v, "section", pairs)

    def pieces(v):
        return [v] + [swap(v, k) for k in range(2, replicas, 2)]

    def everywhere(v):
        return tree(pieces(v + swap(v, 1)))

    *held, copy, x, og, kernel, weight, gain = load(ids, x, og, kernel, weight, gain, height, width, group)
    nexts = [up(copy, True)]
    later = []
    for i in range(1, groups):
        *held, copy = forward(i, x, og, kernel, weight, held, height, width, group)
        later.append(copy)
    depth, pre, raw = held
    raw = add(raw, swap(raw, 1))
    later, raw = lax.optimization_barrier((later, raw))
    raws = pieces(raw)
    nexts += [up(v, False) for v in later]

    recvs, tots, collected = [], [], ()
    for t in range(turns):
        last = t + 1 == turns
        *given, total, pg, dg = turn(
            t, sections, last, ids, og, raws, gain, pre, x, weight, kernel, recvs, tots,
            [] if last or t == 0 else nexts, height, width, count, group,
        )
        if last:
            table, gains, biases, keep, send = terms(
                t, sections, last, ids, x, depth, None, pg, dg, total, collected, height, width
            )
            dg, send = lax.optimization_barrier((dg, send))
            act = finish(t, sections, ids, og, x, dg, kernel, recvs, collected[3:], height, width)
        else:
            fresh, part = given
            recvs = down(fresh, t)
            if t == 0:
                part = cross(fresh, nexts[0])
            tots = down(everywhere(part), t)
            collected = terms(t, sections, last, ids, x, depth, fresh, pg, dg, total, collected, height, width)
            gain, collected = lax.optimization_barrier((gain, collected))
    got = split(ids, keep, send, swap(send, 1), chips)
    recvs = [swap(v, 2 * k) for k, v in enumerate(got[1:], 1)]
    recvs, act = lax.optimization_barrier((recvs, act))
    chunk, table = merge(got[0], recvs)
    half, point = gather(ids, [chunk] + [swap(chunk, 2 * k) for k in range(1, chips)])
    table = table[:9].reshape(1, 3, 3, channels)
    half, table = lax.optimization_barrier((half, table))
    point = widen(ids, swap(half, 1), point)
    return (act.reshape(acts.shape), point[None], table, gains, biases)


def solution(mesh):
    return jax.shard_map(
        body,
        mesh=mesh,
        in_specs=(
            P("section", None, "dp", None, None, None),
            P(None, "dp", None, None, None),
            P("section", None, None, None),
            P("section", None, None),
            P("section", None),
        ),
        out_specs=(
            P("section", None, "dp", None, None, None),
            P("section", None, None),
            P("section", None, None, None),
            P("section", None),
            P("section", None),
        ),
        check_vma=False,
    )
```

```python
import functools

import jax
import jax.numpy as jnp
from jax import lax
from jax.experimental import pallas as pl
from jax.experimental.pallas import tpu as pltpu
from jax.sharding import PartitionSpec as P


epsilon = 1e-05
LANES = 128
F32 = jnp.float32
BF16 = jnp.bfloat16

GROUP = 2
PARAMS = pltpu.CompilerParams(vmem_limit_bytes=16 << 20)


PAD = 8


def pad_shape(height, width, channels):
    return (channels // LANES, height * (width + PAD) + PAD, LANES)


def clear_pad(pad, height, width):
    for h in range(height + 1):
        at = h * (width + PAD)
        pad[:, at : at + PAD, :] = jnp.zeros((pad.shape[0], PAD, LANES), F32)


def put_row(pad, block, h, width, value):
    at = h * (width + PAD) + PAD
    pad[block, at : at + width, :] = value


def three(pad, block, h, width):
    at = h * (width + PAD) + PAD
    return [pad[block, at + d : at + d + width, :] for d in (-1, 0, 1)]


def weighted(taps, cols):
    return taps[0] * cols[0] + taps[1] * cols[1] + taps[2] * cols[2]


def block_loop(channels, work):
    def step(i, carry):
        work(i, pl.ds(pl.multiple_of(i * LANES, LANES), LANES))
        return carry

    lax.fori_loop(0, channels // LANES, step, 0)


def lane_loop(channels, work):
    def step(i, carry):
        work(pl.ds(pl.multiple_of(i * LANES, LANES), LANES))
        return carry

    lax.fori_loop(0, channels // LANES, step, 0)


def kernel_rows(kernel_ref, lanes):
    return [[kernel_ref[i, j : j + 1, lanes].astype(F32) for j in range(3)] for i in range(3)]


def col_sum(v):
    return jnp.sum(v, axis=0, keepdims=True)


VMEM = pl.BlockSpec(memory_space=pltpu.VMEM)
SMEM = pl.BlockSpec(memory_space=pltpu.SMEM)
ANY = pl.BlockSpec(memory_space=pl.ANY)


def forward_group(part, height, width, x_ref, og_ref, kernel_ref, w_ref, depth_ref, pre_ref, raw_ref, copy_ref, pre_s, pad, ready):
    channels = x_ref.shape[-1]
    group = copy_ref.shape[0]
    clear_pad(pad, height, width)

    def one(g, carry):
        slot = part * group + g
        ready(0, slot)

        def conv(block, lanes):
            taps = kernel_rows(kernel_ref, lanes)
            for h in range(height):
                v = x_ref[slot, h * width : (h + 1) * width, lanes].astype(F32)
                put_row(pad, block, h, width, jnp.maximum(v, 0.0))

            def parts(h):
                cols = three(pad, block, h, width)
                return [weighted(taps[i], cols) for i in range(3)]

            window = [None, parts(0), None]
            for h in range(height):
                window[2] = parts(h + 1) if h + 1 < height else None
                total = window[1][1]
                if window[0] is not None:
                    total = total + window[0][0]
                if window[2] is not None:
                    total = total + window[2][2]
                depth_ref[slot, h * width : (h + 1) * width, lanes] = total.astype(BF16)
                window = [window[1], window[2], None]

        block_loop(channels, conv)
        ready(1, slot)
        pre_s[...] = jnp.dot(depth_ref[slot], w_ref[...], preferred_element_type=F32)
        ready(2, slot)

        def sums(lanes):
            p = pre_s[:, lanes]
            v = og_ref[slot, :, lanes].astype(F32)
            short = p.astype(BF16)
            pre_ref[slot, :, lanes] = short
            copy_ref[g, :, lanes] = short
            for row, value in enumerate((p, p * p, v, v * p)):
                raw_ref[slot, row : row + 1, lanes] = col_sum(value)

        lane_loop(channels, sums)
        return carry

    lax.fori_loop(0, group, one, 0)


def load_kernel(height, width, ids, x_far, og_far, kernel_far, w_far, gain_far, *rest):
    depth_ref, pre_ref, raw_ref, copy_ref, x_ref, og_ref, kernel_ref, w_ref, gain_ref, pre_s, pad, few, many = rest
    micros = x_ref.shape[0]
    group = copy_ref.shape[0]
    weights = pltpu.make_async_copy(w_far, w_ref, few.at[0])
    table = pltpu.make_async_copy(kernel_far, kernel_ref, few.at[1])
    gains = pltpu.make_async_copy(gain_far, gain_ref, few.at[2])

    def inputs(m):
        return pltpu.make_async_copy(x_far.at[m], x_ref.at[m], many.at[0, m])

    def outputs(m):
        return pltpu.make_async_copy(og_far.at[m], og_ref.at[m], many.at[1, m])

    table.start()
    for m in range(group):
        inputs(m).start()
        if m == 0:
            weights.start()
    for m in range(group):
        outputs(m).start()

    def ready(stage, slot):
        if stage == 0:
            inputs(slot).wait()

            @pl.when(slot == 0)
            def _():
                table.wait()

        elif stage == 1:

            @pl.when(slot == 0)
            def _():
                weights.wait()
                for m in range(group, micros):
                    inputs(m).start()
                    outputs(m).start()
                gains.start()

        else:
            outputs(slot).wait()

    forward_group(0, height, width, x_ref, og_ref, kernel_ref, w_ref, depth_ref, pre_ref, raw_ref, copy_ref, pre_s, pad, ready)
    for m in range(group, micros):
        inputs(m).wait()
        outputs(m).wait()
    gains.wait()


def load(ids, x, og, kernel, weight, gain, height, width, group):
    micros, rows, channels = x.shape
    table = jax.ShapeDtypeStruct((micros, 4, channels), F32)
    args = [pltpu.with_memory_space_constraint(v, pltpu.HBM) for v in (x, og, kernel, weight, gain)]
    return pl.pallas_call(
        functools.partial(load_kernel, height, width),
        in_specs=[SMEM] + [ANY] * 5,
        out_specs=[VMEM] * 9,
        out_shape=[
            jax.ShapeDtypeStruct(x.shape, BF16),
            jax.ShapeDtypeStruct(x.shape, BF16),
            table,
            jax.ShapeDtypeStruct((group, rows, channels), BF16),
        ]
        + [jax.ShapeDtypeStruct(v.shape, v.dtype) for v in (x, og, kernel, weight, gain)],
        scratch_shapes=[
            pltpu.VMEM((rows, channels), F32),
            pltpu.VMEM(pad_shape(height, width, channels), F32),
            pltpu.SemaphoreType.DMA((3,)),
            pltpu.SemaphoreType.DMA((2, micros)),
        ],
        compiler_params=PARAMS,
        name="load",
    )(ids, *args)


def forward_kernel(part, height, width, x_ref, og_ref, kernel_ref, w_ref, *rest):
    outs = rest[3:]
    group = outs[3].shape[0]
    for old, new in zip(rest[:3], outs):
        new[0 : part * group] = old[0 : part * group]
    forward_group(part, height, width, x_ref, og_ref, kernel_ref, w_ref, *outs, lambda stage, slot: None)


def forward(part, x, og, kernel, weight, held, height, width, group):
    _, rows, channels = x.shape
    return pl.pallas_call(
        functools.partial(forward_kernel, part, height, width),
        in_specs=[VMEM] * 7,
        out_specs=[VMEM] * 4,
        out_shape=[jax.ShapeDtypeStruct(v.shape, v.dtype) for v in held]
        + [jax.ShapeDtypeStruct((group, rows, channels), BF16)],
        input_output_aliases={4 + i: i for i in range(3)},
        scratch_shapes=[
            pltpu.VMEM((rows, channels), F32),
            pltpu.VMEM(pad_shape(height, width, channels), F32),
        ],
        compiler_params=PARAMS,
        name="forward",
    )(x, og, kernel, weight, *held)


def add_kernel(a_ref, b_ref, out_ref):
    out_ref[...] = a_ref[...] + b_ref[...]


def add(a, b):
    return pl.pallas_call(
        add_kernel,
        in_specs=[VMEM, VMEM],
        out_specs=VMEM,
        out_shape=jax.ShapeDtypeStruct(a.shape, a.dtype),
        compiler_params=PARAMS,
        name="add",
    )(a, b)


def chunk_of(t, sections, groups, ids):
    at = t - (sections - 1) + ids[0]
    inside = jnp.clip(at, 0, groups - 1)
    return inside, at == inside


def choose(which, refs, *at):
    value = refs[0][at]
    for i in range(1, len(refs)):
        value = jnp.where(which == i, refs[i][at], value)
    return value


def turn_kernel(t, sections, last, height, width, count, n_recv, n_next, n_raw, n_own, ids, gain_ref, pre_ref, x_ref, w_ref, kernel_ref, *rest):
    raws, rest = rest[:n_raw], rest[n_raw:]
    owns, rest = rest[:n_own], rest[n_own:]
    recvs, tots, nexts = rest[:n_recv], rest[n_recv : 2 * n_recv], rest[2 * n_recv : 2 * n_recv + n_next]
    outs = rest[2 * n_recv + n_next :]
    if last:
        total_out, pg_out, dg_out, rows_s, pads = outs
    else:
        u_out, part_out, total_out, pg_out, dg_out, rows_s, pads = outs
    group, rows, channels = pg_out.shape
    groups = x_ref.shape[0] // group
    place, valid = chunk_of(t, sections, groups, ids)
    top = ids[0] == sections - 1
    side = ids[0] % 2 if n_recv > 1 else 0
    inverse = 1.0 / count

    def upstream(g, line, lanes):
        value = choose(side, recvs, g, line, lanes) if n_recv else None
        if n_own:
            own = owns[0][place * group + g, line, lanes]
            value = jnp.where(top, own, value) if n_recv else own
        return value.astype(F32)

    def before(g):
        slot = place * group + g

        def raw(row):
            return tree([r[slot, row : row + 1, :] for r in raws])

        def reduced(row):
            value = choose(side, tots, g, slice(row, row + 1), slice(None)) if n_recv else None
            if n_own:
                value = jnp.where(top, raw(2 + row), value) if n_recv else raw(2 + row)
            return value

        center = raw(0) * inverse
        square = raw(1) * inverse
        inv = lax.rsqrt(square - center * center + epsilon)
        sum_grad = reduced(0)
        sum_cross = inv * (reduced(1) - center * sum_grad)
        total_out[g, 0:1, :] = sum_cross
        total_out[g, 1:2, :] = sum_grad
        scale = gain_ref[...] * inv
        slope = -scale * inv * sum_cross * inverse
        rows_s[0:1, :] = scale
        rows_s[1:2, :] = slope
        rows_s[2:3, :] = -scale * sum_grad * inverse - slope * center

        def grads(lanes):
            u = upstream(g, slice(None), lanes)
            pre = pre_ref[slot, :, lanes].astype(F32)
            pg_out[g, :, lanes] = (rows_s[0:1, lanes] * u + rows_s[1:2, lanes] * pre + rows_s[2:3, lanes]).astype(BF16)

        lane_loop(channels, grads)

    def after(g, carry):
        slot = place * group + g
        pad = pads.at[g]

        def conv(block, lanes):
            taps = kernel_rows(kernel_ref, lanes)

            def parts(h):
                cols = three(pad, block, h, width)
                dg_out[g, h * width : (h + 1) * width, lanes] = cols[1].astype(BF16)
                return [weighted(taps[i][::-1], cols) for i in range(3)]

            window = [None, parts(0), None]
            first = second = None
            for h in range(height):
                window[2] = parts(h + 1) if h + 1 < height else None
                total = window[1][1]
                if window[0] is not None:
                    total = total + window[0][2]
                if window[2] is not None:
                    total = total + window[2][0]
                window = [window[1], window[2], None]
                line = slice(h * width, (h + 1) * width)
                x = x_ref[slot, line, lanes].astype(F32)
                fresh = (upstream(g, line, lanes) + jnp.where(x > 0.0, total, 0.0)).astype(BF16)
                u_out[g, line, lanes] = fresh
                if n_next:
                    fresh = fresh.astype(F32)
                    mixed = fresh * choose(place, nexts, g, line, lanes).astype(F32)
                    first = fresh if first is None else first + fresh
                    second = mixed if second is None else second + mixed
            if n_next:
                part_out[g, 0:1, lanes] = col_sum(first)
                part_out[g, 1:2, lanes] = col_sum(second)

        block_loop(channels, conv)
        return carry

    @pl.when(valid)
    def _():
        for g in range(group):
            before(g)
        result = lax.dot_general(
            pg_out[...].reshape(group * rows, channels),
            w_ref[...],
            (((1,), (1,)), ((), ())),
            preferred_element_type=F32,
        )
        if last:
            dg_out[...] = result.astype(BF16).reshape(group, rows, channels)
            return
        for g in range(group):
            clear_pad(pads.at[g], height, width)
            for block in range(channels // LANES):
                for h in range(height):
                    line = slice(g * rows + h * width, g * rows + (h + 1) * width)
                    put_row(pads.at[g], block, h, width, result[line, block * LANES : (block + 1) * LANES])
        lax.fori_loop(0, group, after, 0)


def turn(t, sections, last, ids, og, raws, gain, pre, x, weight, kernel, recvs, tots, nexts, height, width, count, group):
    micros, rows, channels = x.shape
    owns = [og] if t < micros // group or not recvs else []
    sent = jax.ShapeDtypeStruct((group, rows, channels), BF16)
    pair = jax.ShapeDtypeStruct((group, 2, channels), F32)
    return pl.pallas_call(
        functools.partial(
            turn_kernel, t, sections, last, height, width, count,
            len(recvs), len(nexts), len(raws), len(owns),
        ),
        in_specs=[SMEM] + [VMEM] * (5 + len(raws) + len(owns) + 2 * len(recvs) + len(nexts)),
        out_specs=[VMEM] * (3 if last else 5),
        scratch_shapes=[
            pltpu.VMEM((8, channels), F32),
            pltpu.VMEM((group, *pad_shape(height, width, channels)), F32),
        ],
        out_shape=([] if last else [sent, pair]) + [pair, sent, sent],
        compiler_params=PARAMS,
        name="turn",
    )(ids, gain, pre, x, weight, kernel, *raws, *owns, *recvs, *tots, *nexts)


def cross_kernel(u_ref, next_ref, out):
    group, _, channels = u_ref.shape
    for g in range(group):

        def sums(lanes):
            u = u_ref[g, :, lanes].astype(F32)
            out[g, 0:1, lanes] = col_sum(u)
            out[g, 1:2, lanes] = col_sum(u * next_ref[g, :, lanes].astype(F32))

        lane_loop(channels, sums)


def cross(u, following):
    group, _, channels = u.shape
    return pl.pallas_call(
        cross_kernel,
        in_specs=[VMEM, VMEM],
        out_specs=VMEM,
        out_shape=jax.ShapeDtypeStruct((group, 2, channels), F32),
        compiler_params=PARAMS,
        name="cross",
    )(u, following)


def added(total_ref, valid, sums_ref):
    extra = total_ref[0]
    for g in range(1, total_ref.shape[0]):
        extra = extra + total_ref[g]
    extra = jnp.where(valid, extra, 0.0)
    return extra if sums_ref is None else sums_ref[...] + extra


def terms_kernel(t, sections, height, width, first, last, ids, x_ref, dg_ref, total_ref, *rest):
    rest, pad = rest[:-1], rest[-1]
    if not last:
        depth_ref, pg_ref, u_ref = rest[:3]
        rest = rest[3:]
    if not first:
        acc_ref = rest[0]
        sums_ref, weight_ref = (None, None) if last else rest[1:3]
        rest = rest[1:] if last else rest[4:]
    else:
        acc_ref = sums_ref = weight_ref = None
    if last:
        (acc_out,) = rest
    else:
        acc_out, sums_out, weight_out, act_out, sem = rest
    group, rows, channels = dg_ref.shape
    groups = x_ref.shape[0] // group
    place, valid = chunk_of(t, sections, groups, ids)
    if not last:

        def moves():
            return pltpu.make_async_copy(u_ref, act_out.at[pl.ds(place * group, group)], sem)

        @pl.when(valid)
        def _():
            moves().start()

    acc_out[...] = jnp.zeros_like(acc_out) if first else acc_ref[...]
    if not last:
        sums_out[...] = added(total_ref, valid, sums_ref)

    def one(g, carry):
        slot = place * group + g

        def terms(block, lanes):
            for h in range(height):
                v = x_ref[slot, h * width : (h + 1) * width, lanes].astype(F32)
                put_row(pad, block, h, width, jnp.maximum(v, 0.0))
            acc = [[None] * 3 for _ in range(3)]
            grads = [None] + [dg_ref[g, h * width : (h + 1) * width, lanes].astype(F32) for h in range(height)] + [None]
            for h in range(height):
                cols = three(pad, block, h, width)
                for i in range(3):
                    up = grads[h + 2 - i]
                    if up is None:
                        continue
                    for j in range(3):
                        p = cols[j] * up
                        acc[i][j] = p if acc[i][j] is None else acc[i][j] + p
            for i in range(3):
                for j in range(3):
                    row = slice(3 * i + j, 3 * i + j + 1)
                    acc_out[row, lanes] += col_sum(acc[i][j])

        block_loop(channels, terms)
        return carry

    @pl.when(valid)
    def _():
        clear_pad(pad, height, width)
        lax.fori_loop(0, group, one, 0)

    if not last:

        @pl.when(valid)
        def _():
            at = pl.ds(place * group, group)
            fresh = lax.dot_general(
                depth_ref[at].reshape(group * rows, channels),
                pg_ref[...].reshape(group * rows, channels),
                (((0,), (0,)), ((), ())),
                preferred_element_type=F32,
            )
            weight_out[...] = fresh if first else weight_ref[...] + fresh

        @pl.when(jnp.logical_not(valid))
        def _():
            weight_out[...] = jnp.zeros_like(weight_out) if first else weight_ref[...]

        @pl.when(valid)
        def _():
            moves().wait()


def terms(t, sections, last, ids, x, depth, u, pg, dg, total, carried, height, width):
    _, _, channels = x.shape
    table = jax.ShapeDtypeStruct((16, channels), F32)
    sums = jax.ShapeDtypeStruct((2, channels), F32)
    square = jax.ShapeDtypeStruct((channels, channels), F32)
    act = jax.ShapeDtypeStruct(x.shape, BF16)
    first = not carried
    if last:
        carried = carried[:1]
        out_shape = [table]
        in_specs = [VMEM] * len(carried)
        out_specs = [VMEM]
        scratch = []
        aliases = {}
    else:
        out_shape = [table, sums, square, act]
        in_specs = [VMEM] * 3 + ([] if first else [VMEM] * 3 + [ANY])
        out_specs = [VMEM, VMEM, VMEM, ANY]
        scratch = [pltpu.SemaphoreType.DMA]
        aliases = {} if first else {9: 2, 10: 3}
        carried = (depth, pg, u, *carried)
    return pl.pallas_call(
        functools.partial(terms_kernel, t, sections, height, width, first, last),
        in_specs=[SMEM] + [VMEM] * 3 + in_specs,
        out_specs=out_specs,
        out_shape=out_shape,
        scratch_shapes=scratch + [pltpu.VMEM(pad_shape(height, width, channels), F32)],
        input_output_aliases=aliases,
        compiler_params=PARAMS,
        name="terms",
    )(ids, x, dg, total, *carried)


def product_kernel(t, sections, micros, ids, depth_ref, pg_ref, *rest):
    keep_out, send_out = rest[-2:]
    group, rows, channels = pg_ref.shape
    place, valid = chunk_of(t, sections, micros // group, ids)
    half = keep_out.shape[0]
    core = ids[1] % 2
    at = pl.ds(place * group, group)
    grads = pg_ref[...].reshape(group * rows, channels)

    def rows_of(side):
        return pl.ds(pl.multiple_of(side * half, half), half)

    def fresh(side):
        return lax.dot_general(
            depth_ref[at, :, rows_of(side)].reshape(group * rows, half),
            grads,
            (((0,), (0,)), ((), ())),
            preferred_element_type=F32,
        )

    def old(side):
        return rest[0][rows_of(side), :] if len(rest) > 2 else jnp.zeros(keep_out.shape, F32)

    @pl.when(valid)
    def _():
        send_out[...] = (old(1 - core) + fresh(1 - core)).astype(BF16)
        keep_out[...] = old(core) + fresh(core)

    @pl.when(jnp.logical_not(valid))
    def _():
        send_out[...] = old(1 - core).astype(BF16)
        keep_out[...] = old(core)


def product(t, sections, ids, depth, pg, carried):
    channels = depth.shape[-1]
    half = channels // 2
    return pl.pallas_call(
        functools.partial(product_kernel, t, sections, depth.shape[0]),
        in_specs=[SMEM] + [VMEM] * (2 + len(carried)),
        out_specs=[VMEM, VMEM],
        out_shape=[
            jax.ShapeDtypeStruct((half, channels), F32),
            jax.ShapeDtypeStruct((half, channels), BF16),
        ],
        compiler_params=PARAMS,
        name="product",
    )(ids, depth, pg, *carried)


def finish_kernel(t, sections, height, width, n_recv, n_own, n_sums, ids, x_ref, dg_ref, kernel_ref, total_ref, *rest):
    owns, rest = rest[:n_own], rest[n_own:]
    recvs, rest = rest[:n_recv], rest[n_recv:]
    act_out, gain_out, bias_out, u_s, pad, sem = rest[-6:]
    group, _, channels = dg_ref.shape
    groups = x_ref.shape[0] // group
    place, valid = chunk_of(t, sections, groups, ids)
    top = ids[0] == sections - 1

    def one(g, carry):
        slot = place * group + g

        def conv(block, lanes):
            taps = kernel_rows(kernel_ref, lanes)
            for h in range(height):
                put_row(pad, block, h, width, dg_ref[g, h * width : (h + 1) * width, lanes].astype(F32))

            def parts(h):
                cols = three(pad, block, h, width)
                return [weighted(taps[i][::-1], cols) for i in range(3)]

            window = [None, parts(0), None]
            for h in range(height):
                window[2] = parts(h + 1) if h + 1 < height else None
                total = window[1][1]
                if window[0] is not None:
                    total = total + window[0][2]
                if window[2] is not None:
                    total = total + window[2][0]
                window = [window[1], window[2], None]
                line = slice(h * width, (h + 1) * width)
                u = recvs[0][g, line, lanes] if n_recv else None
                if n_own:
                    own = owns[0][slot, line, lanes]
                    u = jnp.where(top, own, u) if n_recv else own
                x = x_ref[slot, line, lanes].astype(F32)
                u_s[g, line, lanes] = (u.astype(F32) + jnp.where(x > 0.0, total, 0.0)).astype(BF16)

        block_loop(channels, conv)
        return carry

    sums = added(total_ref, valid, rest[0] if n_sums else None)
    gain_out[...] = sums[0:1]
    bias_out[...] = sums[1:2]

    @pl.when(valid)
    def _():
        clear_pad(pad, height, width)
        lax.fori_loop(0, group, one, 0)
        move = pltpu.make_async_copy(u_s, act_out.at[pl.ds(place * group, group)], sem)
        move.start()
        move.wait()


def finish(t, sections, ids, og, x, dg, kernel, total, recvs, sums, act, height, width):
    owns = [og] if t < x.shape[0] // dg.shape[0] or not recvs else []
    return pl.pallas_call(
        functools.partial(finish_kernel, t, sections, height, width, len(recvs), len(owns), len(sums)),
        in_specs=[SMEM] + [VMEM] * (4 + len(owns) + len(recvs) + len(sums)) + [ANY] * len(act),
        out_specs=[ANY, VMEM, VMEM],
        out_shape=[
            jax.ShapeDtypeStruct(x.shape, BF16),
            jax.ShapeDtypeStruct((1, x.shape[-1]), F32),
            jax.ShapeDtypeStruct((1, x.shape[-1]), F32),
        ],
        scratch_shapes=[
            pltpu.VMEM(dg.shape, BF16),
            pltpu.VMEM(pad_shape(height, width, dg.shape[-1]), F32),
            pltpu.SemaphoreType.DMA,
        ],
        input_output_aliases={5 + len(owns) + len(recvs) + len(sums): 0} if act else {},
        compiler_params=PARAMS,
        name="finish",
    )(ids, x, dg, kernel, total, *owns, *recvs, *sums, *act)


def split_kernel(chips, chunk, where_ref, keep_ref, table_ref, recv_ref, own_out, *outs):
    chip = where_ref[1] // 2
    table = table_ref[...].astype(BF16)
    for k in range(chips):
        at = pl.multiple_of((chip ^ k) * chunk, chunk)
        piece = keep_ref[pl.ds(at, chunk), :] + recv_ref[pl.ds(at, chunk), :].astype(F32)
        if k == 0:
            own_out[0:chunk, :] = piece
            own_out[chunk : chunk + 16, :] = table.astype(F32)
        else:
            outs[k - 1][0:chunk, :] = piece.astype(BF16)
            outs[k - 1][chunk : chunk + 16, :] = table


def split(where, keep, table, recv, chips):
    half, channels = keep.shape
    chunk = half // chips
    return pl.pallas_call(
        functools.partial(split_kernel, chips, chunk),
        in_specs=[SMEM, VMEM, VMEM, VMEM],
        out_specs=[VMEM] * chips,
        out_shape=[jax.ShapeDtypeStruct((chunk + 16, channels), F32)]
        + [jax.ShapeDtypeStruct((chunk + 16, channels), BF16)] * (chips - 1),
        compiler_params=PARAMS,
        name="split",
    )(where, keep, table, recv)


def merge_kernel(chunk, own_ref, *refs):
    parts = tree([own_ref[...]] + [r[...].astype(F32) for r in refs[:-2]])
    refs[-2][...] = parts[0:chunk, :].astype(BF16)
    refs[-1][...] = parts[chunk:, :].astype(BF16)


def merge(own, recvs):
    chunk, channels = own.shape[0] - 16, own.shape[1]
    return pl.pallas_call(
        functools.partial(merge_kernel, chunk),
        in_specs=[VMEM] * (1 + len(recvs)),
        out_specs=[VMEM] * 2,
        out_shape=[
            jax.ShapeDtypeStruct((chunk, channels), BF16),
            jax.ShapeDtypeStruct((16, channels), BF16),
        ],
        compiler_params=PARAMS,
        name="merge",
    )(own, *recvs)


def gather_kernel(chunk, where_ref, table_ref, *refs):
    out = refs[-1]
    for k, ref in enumerate(refs[:-1]):
        at = (where_ref[1] // 2 ^ k) * chunk
        out[pl.ds(pl.multiple_of(at, chunk), chunk), :] = ref[...]
    half = chunk * (len(refs) - 1)
    out[half : half + 16, :] = table_ref[...]


def gather(where, table, parts):
    chunk, channels = parts[0].shape
    half = chunk * len(parts)
    return pl.pallas_call(
        functools.partial(gather_kernel, chunk),
        in_specs=[SMEM] + [VMEM] * (1 + len(parts)),
        out_specs=VMEM,
        out_shape=jax.ShapeDtypeStruct((half + 16, channels), BF16),
        compiler_params=PARAMS,
        name="gather",
    )(where, table, *parts)


def widen_half(source, wide, out_ref, sems, side, pieces=4):
    half = wide.shape[0]
    step = half // pieces
    start = pl.multiple_of(side * half, half)

    def move(i):
        rows = pl.ds(pl.multiple_of(start + i * step, step), step)
        return pltpu.make_async_copy(wide.at[pl.ds(i * step, step)], out_ref.at[rows], sems.at[i])

    for i in range(pieces):
        wide[i * step : (i + 1) * step, :] = source[i * step : (i + 1) * step, :].astype(F32)
        move(i).start()
    for i in range(pieces):
        move(i).wait()


def widen_own_kernel(where_ref, own_ref, out_ref, wide, sems):
    widen_half(own_ref, wide, out_ref, sems, where_ref[1] % 2)


def widen_other_kernel(where_ref, own_ref, recv_ref, out_in, out_ref, table_out, wide, sems, lines, sem):
    half = wide.shape[0]
    both = own_ref[half : half + 16, :].astype(F32) + recv_ref[half : half + 16, :].astype(F32)
    for i in range(9):
        lines[i] = both[i : i + 1, :]
    move = pltpu.make_async_copy(lines, table_out, sem)
    move.start()
    widen_half(recv_ref, wide, out_ref, sems, 1 - where_ref[1] % 2)
    move.wait()


def widen(where, own, recv=None, out=None):
    half, channels = own.shape[0] - 16, own.shape[1]
    point = jax.ShapeDtypeStruct((2 * half, channels), F32)
    scratch = [pltpu.VMEM((half, channels), F32), pltpu.SemaphoreType.DMA((4,))]
    if recv is None:
        return pl.pallas_call(
            widen_own_kernel,
            in_specs=[SMEM, VMEM],
            out_specs=ANY,
            out_shape=point,
            scratch_shapes=scratch,
            compiler_params=PARAMS,
            name="widen_own",
        )(where, own)
    return pl.pallas_call(
        widen_other_kernel,
        in_specs=[SMEM, VMEM, VMEM, ANY],
        out_specs=[ANY, ANY],
        out_shape=[point, jax.ShapeDtypeStruct((9, 1, channels), F32)],
        scratch_shapes=scratch + [pltpu.VMEM((9, 1, channels), F32), pltpu.SemaphoreType.DMA],
        input_output_aliases={3: 0},
        compiler_params=PARAMS,
        name="widen_other",
    )(where, own, recv, out)


def tree(parts):
    while len(parts) > 1:
        parts = [a + b for a, b in zip(parts[::2], parts[1::2])]
    return parts[0]


def body(acts, out_grad, depth_kernel, point_weight, bn_gain):
    sections = lax.axis_size("section")
    replicas = lax.axis_size("dp")
    micros, images, height, width, channels = acts.shape[1:]
    rows = images * height * width
    count = rows * replicas
    chips = replicas // 2
    group = GROUP if micros % GROUP == 0 else 1
    groups = micros // group
    turns = sections + groups - 1
    x = acts.reshape(micros, rows, channels)
    og = out_grad.reshape(micros, rows, channels)
    kernel = depth_kernel[0]
    weight = point_weight[0]
    gain = bn_gain
    ids = jnp.stack([lax.axis_index("section"), lax.axis_index("dp")]).astype(jnp.int32)

    def swap(v, k):
        return lax.ppermute(v, "dp", [(i, i ^ k) for i in range(replicas)])

    def at_work(t):
        return [s for s in range(1, sections) if 0 <= t - (sections - 1 - s) < groups]

    def trade(v):
        return lax.ppermute(v, "section", [(s, s ^ 1) for s in range(sections)])

    def down(v, t):
        if t == 0:
            return [lax.ppermute(v, "section", [(s, s - 1) for s in at_work(t)])]
        if sections % 2 == 0 and all(s % 2 for s in at_work(t)):
            return [trade(v)]
        return [lax.ppermute(v, "section", [(s, (s - 1) % sections) for s in range(sections)])]

    def up(v, wrap):
        pairs = [(s, (s + 1) % sections) for s in range(sections if wrap else sections - 1)]
        return lax.ppermute(v, "section", pairs)

    def pieces(v):
        return [v] + [swap(v, k) for k in range(2, replicas, 2)]

    *held, copy, x, og, kernel, weight, gain = load(ids, x, og, kernel, weight, gain, height, width, group)
    nexts = [up(copy, True)]
    later = []
    for i in range(1, groups):
        *held, copy = forward(i, x, og, kernel, weight, held, height, width, group)
        later.append(copy)
    depth, pre, raw = held
    raw = add(raw, swap(raw, 1))
    later, raw = lax.optimization_barrier((later, raw))
    raws = pieces(raw)
    nexts += [up(v, False) for v in later]

    recvs, tots, collected = [], [], ()
    for t in range(turns):
        last = t + 1 == turns
        *given, total, pg, dg = turn(
            t, sections, last, ids, og, raws, gain, pre, x, weight, kernel, recvs, tots,
            [] if last or t == 0 else nexts, height, width, count, group,
        )
        if last:
            keep, send = product(t, sections, ids, depth, pg, collected[2:3])
            dg, send = lax.optimization_barrier((dg, send))
            (table,) = terms(
                t, sections, last, ids, x, depth, None, pg, dg, total, collected, height, width
            )
            dg, table = lax.optimization_barrier((dg, table))
            act, gains, biases = finish(
                t, sections, ids, og, x, dg, kernel, total, recvs, collected[1:2], collected[3:], height, width
            )
        else:
            fresh, part = given
            recvs = down(fresh, t)
            if t == 0:
                part = cross(fresh, nexts[0])
            other = swap(part, 1)
            tots = down(tree(pieces(part + other)), t)
            collected = terms(t, sections, last, ids, x, depth, fresh, pg, dg, total, collected, height, width)
            gain, collected = lax.optimization_barrier((gain, collected))
    got = split(ids, keep, table, swap(send, 1), chips)
    recvs = [swap(v, 2 * k) for k, v in enumerate(got[1:], 1)]
    recvs, act = lax.optimization_barrier((recvs, act))
    chunk, table = merge(got[0], recvs)
    half = gather(ids, table, [chunk] + [swap(chunk, 2 * k) for k in range(1, chips)])
    point, table = widen(ids, half, swap(half, 1), widen(ids, half))
    table = table.reshape(3, 3, 1, channels).transpose(2, 0, 1, 3)
    return (act.reshape(acts.shape), point[None], table, gains, biases)


def solution(mesh):
    return jax.shard_map(
        body,
        mesh=mesh,
        in_specs=(
            P("section", None, "dp", None, None, None),
            P(None, "dp", None, None, None),
            P("section", None, None, None),
            P("section", None, None),
            P("section", None),
        ),
        out_specs=(
            P("section", None, "dp", None, None, None),
            P("section", None, None),
            P("section", None, None, None),
            P("section", None),
            P("section", None),
        ),
        check_vma=False,
    )
```

```python
import functools

import jax
import jax.numpy as jnp
from jax import lax
from jax.experimental import pallas as pl
from jax.experimental.pallas import tpu as pltpu
from jax.sharding import PartitionSpec as P


epsilon = 1e-05
LANES = 128
F32 = jnp.float32
BF16 = jnp.bfloat16

GROUP = 2
PARAMS = pltpu.CompilerParams(vmem_limit_bytes=16 << 20)


PAD = 8


def pad_shape(height, width, channels):
    return (channels // LANES, height * (width + PAD) + PAD, LANES)


def clear_pad(pad, height, width):
    for h in range(height + 1):
        at = h * (width + PAD)
        pad[:, at : at + PAD, :] = jnp.zeros((pad.shape[0], PAD, LANES), F32)


def put_row(pad, block, h, width, value):
    at = h * (width + PAD) + PAD
    pad[block, at : at + width, :] = value


def three(pad, block, h, width):
    at = h * (width + PAD) + PAD
    return [pad[block, at + d : at + d + width, :] for d in (-1, 0, 1)]


def weighted(taps, cols):
    return taps[0] * cols[0] + taps[1] * cols[1] + taps[2] * cols[2]


def block_loop(channels, work):
    def step(i, carry):
        work(i, pl.ds(pl.multiple_of(i * LANES, LANES), LANES))
        return carry

    lax.fori_loop(0, channels // LANES, step, 0)


def lane_loop(channels, work):
    def step(i, carry):
        work(pl.ds(pl.multiple_of(i * LANES, LANES), LANES))
        return carry

    lax.fori_loop(0, channels // LANES, step, 0)


def kernel_rows(kernel_ref, lanes):
    return [[kernel_ref[i, j : j + 1, lanes].astype(F32) for j in range(3)] for i in range(3)]


def col_sum(v):
    return jnp.sum(v, axis=0, keepdims=True)


VMEM = pl.BlockSpec(memory_space=pltpu.VMEM)
SMEM = pl.BlockSpec(memory_space=pltpu.SMEM)
ANY = pl.BlockSpec(memory_space=pl.ANY)


def forward_group(part, height, width, x_ref, og_ref, kernel_ref, w_ref, depth_ref, pre_ref, raw_ref, copy_ref, pre_s, pad, ready):
    channels = x_ref.shape[-1]
    group = copy_ref.shape[0]
    clear_pad(pad, height, width)

    def one(g, carry):
        slot = part * group + g
        ready(0, slot)

        def conv(block, lanes):
            taps = kernel_rows(kernel_ref, lanes)
            for h in range(height):
                v = x_ref[slot, h * width : (h + 1) * width, lanes].astype(F32)
                put_row(pad, block, h, width, jnp.maximum(v, 0.0))

            def parts(h):
                cols = three(pad, block, h, width)
                return [weighted(taps[i], cols) for i in range(3)]

            window = [None, parts(0), None]
            for h in range(height):
                window[2] = parts(h + 1) if h + 1 < height else None
                total = window[1][1]
                if window[0] is not None:
                    total = total + window[0][0]
                if window[2] is not None:
                    total = total + window[2][2]
                depth_ref[slot, h * width : (h + 1) * width, lanes] = total.astype(BF16)
                window = [window[1], window[2], None]

        block_loop(channels, conv)
        ready(1, slot)
        pre_s[...] = jnp.dot(depth_ref[slot], w_ref[...], preferred_element_type=F32)
        ready(2, slot)

        def sums(lanes):
            p = pre_s[:, lanes]
            v = og_ref[slot, :, lanes].astype(F32)
            short = p.astype(BF16)
            pre_ref[slot, :, lanes] = short
            copy_ref[g, :, lanes] = short
            for row, value in enumerate((p, p * p, v, v * p)):
                raw_ref[g, row : row + 1, lanes] = col_sum(value)

        lane_loop(channels, sums)
        return carry

    lax.fori_loop(0, group, one, 0)


def load_kernel(height, width, ids, x_far, og_far, kernel_far, w_far, gain_far, *rest):
    depth_ref, pre_ref, raw_ref, copy_ref, x_ref, og_ref, kernel_ref, w_ref, gain_ref, pre_s, pad, few, many = rest
    micros = x_ref.shape[0]
    group = copy_ref.shape[0]
    weights = pltpu.make_async_copy(w_far, w_ref, few.at[0])
    table = pltpu.make_async_copy(kernel_far, kernel_ref, few.at[1])
    gains = pltpu.make_async_copy(gain_far, gain_ref, few.at[2])

    def inputs(m):
        return pltpu.make_async_copy(x_far.at[m], x_ref.at[m], many.at[0, m])

    def outputs(m):
        return pltpu.make_async_copy(og_far.at[m], og_ref.at[m], many.at[1, m])

    table.start()
    for m in range(group):
        inputs(m).start()
        if m == 0:
            weights.start()
    for m in range(group):
        outputs(m).start()

    def ready(stage, slot):
        if stage == 0:
            inputs(slot).wait()

            @pl.when(slot == 0)
            def _():
                table.wait()

        elif stage == 1:

            @pl.when(slot == 0)
            def _():
                weights.wait()
                for m in range(group, micros):
                    inputs(m).start()
                    outputs(m).start()
                gains.start()

        else:
            outputs(slot).wait()

    forward_group(0, height, width, x_ref, og_ref, kernel_ref, w_ref, depth_ref, pre_ref, raw_ref, copy_ref, pre_s, pad, ready)
    for m in range(group, micros):
        inputs(m).wait()
        outputs(m).wait()
    gains.wait()


def load(ids, x, og, kernel, weight, gain, height, width, group):
    micros, rows, channels = x.shape
    table = jax.ShapeDtypeStruct((group, 4, channels), F32)
    args = [pltpu.with_memory_space_constraint(v, pltpu.HBM) for v in (x, og, kernel, weight, gain)]
    return pl.pallas_call(
        functools.partial(load_kernel, height, width),
        in_specs=[SMEM] + [ANY] * 5,
        out_specs=[VMEM] * 9,
        out_shape=[
            jax.ShapeDtypeStruct(x.shape, BF16),
            jax.ShapeDtypeStruct(x.shape, BF16),
            table,
            jax.ShapeDtypeStruct((group, rows, channels), BF16),
        ]
        + [jax.ShapeDtypeStruct(v.shape, v.dtype) for v in (x, og, kernel, weight, gain)],
        scratch_shapes=[
            pltpu.VMEM((rows, channels), F32),
            pltpu.VMEM(pad_shape(height, width, channels), F32),
            pltpu.SemaphoreType.DMA((3,)),
            pltpu.SemaphoreType.DMA((2, micros)),
        ],
        compiler_params=PARAMS,
        name="load",
    )(ids, *args)


def forward_kernel(part, height, width, x_ref, og_ref, kernel_ref, w_ref, *rest):
    outs = rest[2:]
    group = outs[3].shape[0]
    for old, new in zip(rest[:2], outs):
        new[0 : part * group] = old[0 : part * group]
    forward_group(part, height, width, x_ref, og_ref, kernel_ref, w_ref, *outs, lambda stage, slot: None)


def forward(part, x, og, kernel, weight, held, height, width, group):
    _, rows, channels = x.shape
    return pl.pallas_call(
        functools.partial(forward_kernel, part, height, width),
        in_specs=[VMEM] * 6,
        out_specs=[VMEM] * 4,
        out_shape=[jax.ShapeDtypeStruct(v.shape, v.dtype) for v in held]
        + [
            jax.ShapeDtypeStruct((group, 4, channels), F32),
            jax.ShapeDtypeStruct((group, rows, channels), BF16),
        ],
        input_output_aliases={4: 0, 5: 1},
        scratch_shapes=[
            pltpu.VMEM((rows, channels), F32),
            pltpu.VMEM(pad_shape(height, width, channels), F32),
        ],
        compiler_params=PARAMS,
        name="forward",
    )(x, og, kernel, weight, *held)


def add_kernel(a_ref, b_ref, out_ref):
    out_ref[...] = a_ref[...] + b_ref[...]


def add(a, b):
    return pl.pallas_call(
        add_kernel,
        in_specs=[VMEM, VMEM],
        out_specs=VMEM,
        out_shape=jax.ShapeDtypeStruct(a.shape, a.dtype),
        compiler_params=PARAMS,
        name="add",
    )(a, b)


def chunk_of(t, sections, groups, ids):
    at = t - (sections - 1) + ids[0]
    inside = jnp.clip(at, 0, groups - 1)
    return inside, at == inside


def choose(which, refs, *at):
    value = refs[0][at]
    for i in range(1, len(refs)):
        value = jnp.where(which == i, refs[i][at], value)
    return value


def turn_kernel(t, sections, last, height, width, count, n_recv, n_next, starts, n_raws, n_own, n_idle, ids, gain_ref, pre_ref, x_ref, w_ref, kernel_ref, *rest):
    raws = []
    for n in n_raws:
        raws.append(rest[:n])
        rest = rest[n:]
    owns, rest = rest[:n_own], rest[n_own:]
    idles, rest = rest[:n_idle], rest[n_idle:]
    recvs, tots, nexts = rest[:n_recv], rest[n_recv : 2 * n_recv], rest[2 * n_recv : 2 * n_recv + n_next]
    outs = rest[2 * n_recv + n_next :]
    if last:
        total_out, pg_out, dg_out, rows_s, pads = outs
    else:
        u_out, part_out, total_out, pg_out, dg_out, rows_s, pads = outs
    group, rows, channels = pg_out.shape
    groups = x_ref.shape[0] // group
    place, valid = chunk_of(t, sections, groups, ids)
    top = ids[0] == sections - 1
    side = ids[0] % 2 if n_recv > 1 else 0
    which = place if n_next <= groups else jnp.where(place == 0, 0, 2 - ids[0] % 2)
    inverse = 1.0 / count

    def upstream(g, line, lanes):
        value = choose(side, recvs, g, line, lanes) if n_recv else None
        if n_own:
            own = owns[0][place * group + g, line, lanes]
            value = jnp.where(top, own, value) if n_recv else own
        return value.astype(F32)

    def before(g):
        slot = place * group + g

        def raw(row):
            values = [
                tree([r[g, start + row : start + row + 1, :] for r in refs])
                for refs, start in zip(raws, starts)
            ]
            value = values[0]
            for i in range(1, len(values)):
                value = jnp.where(place == i, values[i], value)
            return value

        def reduced(row):
            value = choose(side, tots, g, slice(row, row + 1), slice(None)) if n_recv else None
            if n_own:
                value = jnp.where(top, raw(2 + row), value) if n_recv else raw(2 + row)
            return value

        center = raw(0) * inverse
        square = raw(1) * inverse
        inv = lax.rsqrt(square - center * center + epsilon)
        sum_grad = reduced(0)
        sum_cross = inv * (reduced(1) - center * sum_grad)
        total_out[g, 0:1, :] = sum_cross
        total_out[g, 1:2, :] = sum_grad
        scale = gain_ref[...] * inv
        slope = -scale * inv * sum_cross * inverse
        rows_s[0:1, :] = scale
        rows_s[1:2, :] = slope
        rows_s[2:3, :] = -scale * sum_grad * inverse - slope * center

        def grads(lanes):
            u = upstream(g, slice(None), lanes)
            pre = pre_ref[slot, :, lanes].astype(F32)
            pg_out[g, :, lanes] = (rows_s[0:1, lanes] * u + rows_s[1:2, lanes] * pre + rows_s[2:3, lanes]).astype(BF16)

        lane_loop(channels, grads)

    def after(g, carry):
        slot = place * group + g
        pad = pads.at[g]

        def conv(block, lanes):
            taps = kernel_rows(kernel_ref, lanes)

            def parts(h):
                cols = three(pad, block, h, width)
                dg_out[g, h * width : (h + 1) * width, lanes] = cols[1].astype(BF16)
                return [weighted(taps[i][::-1], cols) for i in range(3)]

            window = [None, parts(0), None]
            first = second = None
            for h in range(height):
                window[2] = parts(h + 1) if h + 1 < height else None
                total = window[1][1]
                if window[0] is not None:
                    total = total + window[0][2]
                if window[2] is not None:
                    total = total + window[2][0]
                window = [window[1], window[2], None]
                line = slice(h * width, (h + 1) * width)
                x = x_ref[slot, line, lanes].astype(F32)
                fresh = (upstream(g, line, lanes) + jnp.where(x > 0.0, total, 0.0)).astype(BF16)
                u_out[g, line, lanes] = fresh
                if n_next:
                    fresh = fresh.astype(F32)
                    mixed = fresh * choose(which, nexts, g, line, lanes).astype(F32)
                    first = fresh if first is None else first + fresh
                    second = mixed if second is None else second + mixed
            if n_next:
                part_out[g, 0:1, lanes] = col_sum(first)
                part_out[g, 1:2, lanes] = col_sum(second)

        block_loop(channels, conv)
        return carry

    @pl.when(valid)
    def _():
        for g in range(group):
            before(g)
        result = lax.dot_general(
            pg_out[...].reshape(group * rows, channels),
            w_ref[...],
            (((1,), (1,)), ((), ())),
            preferred_element_type=F32,
        )
        if last:
            dg_out[...] = result.astype(BF16).reshape(group, rows, channels)
            return
        for g in range(group):
            clear_pad(pads.at[g], height, width)
            for block in range(channels // LANES):
                for h in range(height):
                    line = slice(g * rows + h * width, g * rows + (h + 1) * width)
                    put_row(pads.at[g], block, h, width, result[line, block * LANES : (block + 1) * LANES])
        lax.fori_loop(0, group, after, 0)

    if n_idle:

        @pl.when(jnp.logical_not(valid))
        def _():
            u_out[...] = idles[0][...]


def turn(t, sections, last, ids, og, raws, starts, gain, pre, x, weight, kernel, recvs, tots, nexts, idles, height, width, count, group):
    micros, rows, channels = x.shape
    flat = [v for r in raws for v in r]
    owns = [og] if t < micros // group or not recvs else []
    sent = jax.ShapeDtypeStruct((group, rows, channels), BF16)
    pair = jax.ShapeDtypeStruct((group, 2, channels), F32)
    return pl.pallas_call(
        functools.partial(
            turn_kernel, t, sections, last, height, width, count,
            len(recvs), len(nexts), starts, [len(r) for r in raws], len(owns), len(idles),
        ),
        in_specs=[SMEM] + [VMEM] * (5 + len(flat) + len(owns) + len(idles) + 2 * len(recvs) + len(nexts)),
        out_specs=[VMEM] * (3 if last else 5),
        scratch_shapes=[
            pltpu.VMEM((8, channels), F32),
            pltpu.VMEM((group, *pad_shape(height, width, channels)), F32),
        ],
        out_shape=([] if last else [sent, pair]) + [pair, sent, sent],
        compiler_params=PARAMS,
        name="turn",
    )(ids, gain, pre, x, weight, kernel, *flat, *owns, *idles, *recvs, *tots, *nexts)


def cross_kernel(u_ref, next_ref, *rest):
    out = rest[-1]
    group, _, channels = u_ref.shape
    if len(rest) > 1:
        out[:, 2:, :] = rest[0][...]
    for g in range(group):

        def sums(lanes):
            u = u_ref[g, :, lanes].astype(F32)
            out[g, 0:1, lanes] = col_sum(u)
            out[g, 1:2, lanes] = col_sum(u * next_ref[g, :, lanes].astype(F32))

        lane_loop(channels, sums)


def cross(u, following, riders):
    group, _, channels = u.shape
    return pl.pallas_call(
        cross_kernel,
        in_specs=[VMEM] * (2 + len(riders)),
        out_specs=VMEM,
        out_shape=jax.ShapeDtypeStruct((group, 6 if riders else 2, channels), F32),
        compiler_params=PARAMS,
        name="cross",
    )(u, following, *riders)


def added(total_ref, valid, sums_ref):
    extra = total_ref[0]
    for g in range(1, total_ref.shape[0]):
        extra = extra + total_ref[g]
    extra = jnp.where(valid, extra, 0.0)
    return extra if sums_ref is None else sums_ref[...] + extra


def terms_kernel(t, sections, height, width, first, last, ids, x_ref, dg_ref, total_ref, *rest):
    rest, pad = rest[:-1], rest[-1]
    if not last:
        depth_ref, pg_ref, u_ref = rest[:3]
        rest = rest[3:]
    if not first:
        acc_ref = rest[0]
        sums_ref, weight_ref = (None, None) if last else rest[1:3]
        rest = rest[1:] if last else rest[4:]
    else:
        acc_ref = sums_ref = weight_ref = None
    if last:
        (acc_out,) = rest
    else:
        acc_out, sums_out, weight_out, act_out, sem = rest
    group, rows, channels = dg_ref.shape
    groups = x_ref.shape[0] // group
    place, valid = chunk_of(t, sections, groups, ids)
    if not last:

        def moves():
            return pltpu.make_async_copy(u_ref, act_out.at[pl.ds(place * group, group)], sem)

        @pl.when(valid)
        def _():
            moves().start()

    acc_out[...] = jnp.zeros_like(acc_out) if first else acc_ref[...]
    if not last:
        sums_out[...] = added(total_ref, valid, sums_ref)

    def one(g, carry):
        slot = place * group + g

        def terms(block, lanes):
            for h in range(height):
                v = x_ref[slot, h * width : (h + 1) * width, lanes].astype(F32)
                put_row(pad, block, h, width, jnp.maximum(v, 0.0))
            acc = [[None] * 3 for _ in range(3)]
            grads = [None] + [dg_ref[g, h * width : (h + 1) * width, lanes].astype(F32) for h in range(height)] + [None]
            for h in range(height):
                cols = three(pad, block, h, width)
                for i in range(3):
                    up = grads[h + 2 - i]
                    if up is None:
                        continue
                    for j in range(3):
                        p = cols[j] * up
                        acc[i][j] = p if acc[i][j] is None else acc[i][j] + p
            for i in range(3):
                for j in range(3):
                    row = slice(3 * i + j, 3 * i + j + 1)
                    acc_out[row, lanes] += col_sum(acc[i][j])

        block_loop(channels, terms)
        return carry

    @pl.when(valid)
    def _():
        clear_pad(pad, height, width)
        lax.fori_loop(0, group, one, 0)

    if not last:

        @pl.when(valid)
        def _():
            at = pl.ds(place * group, group)
            fresh = lax.dot_general(
                depth_ref[at].reshape(group * rows, channels),
                pg_ref[...].reshape(group * rows, channels),
                (((0,), (0,)), ((), ())),
                preferred_element_type=F32,
            )
            weight_out[...] = fresh if first else weight_ref[...] + fresh

        @pl.when(jnp.logical_not(valid))
        def _():
            weight_out[...] = jnp.zeros_like(weight_out) if first else weight_ref[...]

        @pl.when(valid)
        def _():
            moves().wait()


def terms(t, sections, last, ids, x, depth, u, pg, dg, total, carried, height, width):
    _, _, channels = x.shape
    table = jax.ShapeDtypeStruct((16, channels), F32)
    sums = jax.ShapeDtypeStruct((2, channels), F32)
    square = jax.ShapeDtypeStruct((channels, channels), F32)
    act = jax.ShapeDtypeStruct(x.shape, BF16)
    first = not carried
    if last:
        carried = carried[:1]
        out_shape = [table]
        in_specs = [VMEM] * len(carried)
        out_specs = [VMEM]
        scratch = []
        aliases = {}
    else:
        out_shape = [table, sums, square, act]
        in_specs = [VMEM] * 3 + ([] if first else [VMEM] * 3 + [ANY])
        out_specs = [VMEM, VMEM, VMEM, ANY]
        scratch = [pltpu.SemaphoreType.DMA]
        aliases = {} if first else {9: 2, 10: 3}
        carried = (depth, pg, u, *carried)
    return pl.pallas_call(
        functools.partial(terms_kernel, t, sections, height, width, first, last),
        in_specs=[SMEM] + [VMEM] * 3 + in_specs,
        out_specs=out_specs,
        out_shape=out_shape,
        scratch_shapes=scratch + [pltpu.VMEM(pad_shape(height, width, channels), F32)],
        input_output_aliases=aliases,
        compiler_params=PARAMS,
        name="terms",
    )(ids, x, dg, total, *carried)


def product_kernel(t, sections, micros, ids, depth_ref, pg_ref, *rest):
    keep_out, send_out = rest[-2:]
    group, rows, channels = pg_ref.shape
    place, valid = chunk_of(t, sections, micros // group, ids)
    half = keep_out.shape[0]
    core = ids[1] % 2
    at = pl.ds(place * group, group)
    grads = pg_ref[...].reshape(group * rows, channels)

    def rows_of(side):
        return pl.ds(pl.multiple_of(side * half, half), half)

    def fresh(side):
        return lax.dot_general(
            depth_ref[at, :, rows_of(side)].reshape(group * rows, half),
            grads,
            (((0,), (0,)), ((), ())),
            preferred_element_type=F32,
        )

    def old(side):
        return rest[0][rows_of(side), :] if len(rest) > 2 else jnp.zeros(keep_out.shape, F32)

    @pl.when(valid)
    def _():
        send_out[...] = (old(1 - core) + fresh(1 - core)).astype(BF16)
        keep_out[...] = old(core) + fresh(core)

    @pl.when(jnp.logical_not(valid))
    def _():
        send_out[...] = old(1 - core).astype(BF16)
        keep_out[...] = old(core)


def product(t, sections, ids, depth, pg, carried):
    channels = depth.shape[-1]
    half = channels // 2
    return pl.pallas_call(
        functools.partial(product_kernel, t, sections, depth.shape[0]),
        in_specs=[SMEM] + [VMEM] * (2 + len(carried)),
        out_specs=[VMEM, VMEM],
        out_shape=[
            jax.ShapeDtypeStruct((half, channels), F32),
            jax.ShapeDtypeStruct((half, channels), BF16),
        ],
        compiler_params=PARAMS,
        name="product",
    )(ids, depth, pg, *carried)


def finish_kernel(t, sections, height, width, n_recv, n_own, n_sums, ids, x_ref, dg_ref, kernel_ref, total_ref, *rest):
    owns, rest = rest[:n_own], rest[n_own:]
    recvs, rest = rest[:n_recv], rest[n_recv:]
    act_out, gain_out, bias_out, u_s, pad, sem = rest[-6:]
    group, _, channels = dg_ref.shape
    groups = x_ref.shape[0] // group
    place, valid = chunk_of(t, sections, groups, ids)
    top = ids[0] == sections - 1

    def one(g, carry):
        slot = place * group + g

        def conv(block, lanes):
            taps = kernel_rows(kernel_ref, lanes)
            for h in range(height):
                put_row(pad, block, h, width, dg_ref[g, h * width : (h + 1) * width, lanes].astype(F32))

            def parts(h):
                cols = three(pad, block, h, width)
                return [weighted(taps[i][::-1], cols) for i in range(3)]

            window = [None, parts(0), None]
            for h in range(height):
                window[2] = parts(h + 1) if h + 1 < height else None
                total = window[1][1]
                if window[0] is not None:
                    total = total + window[0][2]
                if window[2] is not None:
                    total = total + window[2][0]
                window = [window[1], window[2], None]
                line = slice(h * width, (h + 1) * width)
                u = recvs[0][g, line, lanes] if n_recv else None
                if n_own:
                    own = owns[0][slot, line, lanes]
                    u = jnp.where(top, own, u) if n_recv else own
                x = x_ref[slot, line, lanes].astype(F32)
                u_s[g, line, lanes] = (u.astype(F32) + jnp.where(x > 0.0, total, 0.0)).astype(BF16)

        block_loop(channels, conv)
        return carry

    sums = added(total_ref, valid, rest[0] if n_sums else None)
    gain_out[...] = sums[0:1]
    bias_out[...] = sums[1:2]

    @pl.when(valid)
    def _():
        clear_pad(pad, height, width)
        lax.fori_loop(0, group, one, 0)
        move = pltpu.make_async_copy(u_s, act_out.at[pl.ds(place * group, group)], sem)
        move.start()
        move.wait()


def finish(t, sections, ids, og, x, dg, kernel, total, recvs, sums, act, height, width):
    owns = [og] if t < x.shape[0] // dg.shape[0] or not recvs else []
    return pl.pallas_call(
        functools.partial(finish_kernel, t, sections, height, width, len(recvs), len(owns), len(sums)),
        in_specs=[SMEM] + [VMEM] * (4 + len(owns) + len(recvs) + len(sums)) + [ANY] * len(act),
        out_specs=[ANY, VMEM, VMEM],
        out_shape=[
            jax.ShapeDtypeStruct(x.shape, BF16),
            jax.ShapeDtypeStruct((1, x.shape[-1]), F32),
            jax.ShapeDtypeStruct((1, x.shape[-1]), F32),
        ],
        scratch_shapes=[
            pltpu.VMEM(dg.shape, BF16),
            pltpu.VMEM(pad_shape(height, width, dg.shape[-1]), F32),
            pltpu.SemaphoreType.DMA,
        ],
        input_output_aliases={5 + len(owns) + len(recvs) + len(sums): 0} if act else {},
        compiler_params=PARAMS,
        name="finish",
    )(ids, x, dg, kernel, total, *owns, *recvs, *sums, *act)


def split_kernel(chips, chunk, where_ref, keep_ref, table_ref, recv_ref, own_out, *outs):
    chip = where_ref[1] // 2
    table = table_ref[...].astype(BF16)
    for k in range(chips):
        at = pl.multiple_of((chip ^ k) * chunk, chunk)
        piece = keep_ref[pl.ds(at, chunk), :] + recv_ref[pl.ds(at, chunk), :].astype(F32)
        if k == 0:
            own_out[0:chunk, :] = piece
            own_out[chunk : chunk + 16, :] = table.astype(F32)
        else:
            outs[k - 1][0:chunk, :] = piece.astype(BF16)
            outs[k - 1][chunk : chunk + 16, :] = table


def split(where, keep, table, recv, chips):
    half, channels = keep.shape
    chunk = half // chips
    return pl.pallas_call(
        functools.partial(split_kernel, chips, chunk),
        in_specs=[SMEM, VMEM, VMEM, VMEM],
        out_specs=[VMEM] * chips,
        out_shape=[jax.ShapeDtypeStruct((chunk + 16, channels), F32)]
        + [jax.ShapeDtypeStruct((chunk + 16, channels), BF16)] * (chips - 1),
        compiler_params=PARAMS,
        name="split",
    )(where, keep, table, recv)


def merge_kernel(chunk, own_ref, *refs):
    parts = tree([own_ref[...]] + [r[...].astype(F32) for r in refs[:-2]])
    refs[-2][...] = parts[0:chunk, :].astype(BF16)
    refs[-1][...] = parts[chunk:, :].astype(BF16)


def merge(own, recvs):
    chunk, channels = own.shape[0] - 16, own.shape[1]
    return pl.pallas_call(
        functools.partial(merge_kernel, chunk),
        in_specs=[VMEM] * (1 + len(recvs)),
        out_specs=[VMEM] * 2,
        out_shape=[
            jax.ShapeDtypeStruct((chunk, channels), BF16),
            jax.ShapeDtypeStruct((16, channels), BF16),
        ],
        compiler_params=PARAMS,
        name="merge",
    )(own, *recvs)


def gather_kernel(chunk, where_ref, table_ref, *refs):
    out = refs[-1]
    for k, ref in enumerate(refs[:-1]):
        at = (where_ref[1] // 2 ^ k) * chunk
        out[pl.ds(pl.multiple_of(at, chunk), chunk), :] = ref[...]
    half = chunk * (len(refs) - 1)
    out[half : half + 16, :] = table_ref[...]


def gather(where, table, parts):
    chunk, channels = parts[0].shape
    half = chunk * len(parts)
    return pl.pallas_call(
        functools.partial(gather_kernel, chunk),
        in_specs=[SMEM] + [VMEM] * (1 + len(parts)),
        out_specs=VMEM,
        out_shape=jax.ShapeDtypeStruct((half + 16, channels), BF16),
        compiler_params=PARAMS,
        name="gather",
    )(where, table, *parts)


def widen_half(source, wide, out_ref, sems, side, pieces=8):
    half = wide.shape[0]
    step = half // pieces
    start = pl.multiple_of(side * half, half)

    def move(i):
        rows = pl.ds(pl.multiple_of(start + i * step, step), step)
        return pltpu.make_async_copy(wide.at[pl.ds(i * step, step)], out_ref.at[rows], sems.at[i])

    for i in range(pieces):
        wide[i * step : (i + 1) * step, :] = source[i * step : (i + 1) * step, :].astype(F32)
        move(i).start()
    for i in range(pieces):
        move(i).wait()


def widen_own_kernel(where_ref, own_ref, out_ref, wide, sems):
    widen_half(own_ref, wide, out_ref, sems, where_ref[1] % 2)


def widen_other_kernel(where_ref, own_ref, recv_ref, out_in, out_ref, table_out, wide, sems, lines, sem):
    half = wide.shape[0]
    both = own_ref[half : half + 16, :].astype(F32) + recv_ref[half : half + 16, :].astype(F32)
    for i in range(9):
        lines[i] = both[i : i + 1, :]
    move = pltpu.make_async_copy(lines, table_out, sem)
    move.start()
    widen_half(recv_ref, wide, out_ref, sems, 1 - where_ref[1] % 2)
    move.wait()


def widen(where, own, recv=None, out=None):
    half, channels = own.shape[0] - 16, own.shape[1]
    point = jax.ShapeDtypeStruct((2 * half, channels), F32)
    scratch = [pltpu.VMEM((half, channels), F32), pltpu.SemaphoreType.DMA((8,))]
    if recv is None:
        return pl.pallas_call(
            widen_own_kernel,
            in_specs=[SMEM, VMEM],
            out_specs=ANY,
            out_shape=point,
            scratch_shapes=scratch,
            compiler_params=PARAMS,
            name="widen_own",
        )(where, own)
    return pl.pallas_call(
        widen_other_kernel,
        in_specs=[SMEM, VMEM, VMEM, ANY],
        out_specs=[ANY, ANY],
        out_shape=[point, jax.ShapeDtypeStruct((9, 1, channels), F32)],
        scratch_shapes=scratch + [pltpu.VMEM((9, 1, channels), F32), pltpu.SemaphoreType.DMA],
        input_output_aliases={3: 0},
        compiler_params=PARAMS,
        name="widen_other",
    )(where, own, recv, out)


def tree(parts):
    while len(parts) > 1:
        parts = [a + b for a, b in zip(parts[::2], parts[1::2])]
    return parts[0]


def body(acts, out_grad, depth_kernel, point_weight, bn_gain):
    sections = lax.axis_size("section")
    replicas = lax.axis_size("dp")
    micros, images, height, width, channels = acts.shape[1:]
    rows = images * height * width
    count = rows * replicas
    chips = replicas // 2
    group = GROUP if micros % GROUP == 0 else 1
    groups = micros // group
    turns = sections + groups - 1
    x = acts.reshape(micros, rows, channels)
    og = out_grad.reshape(micros, rows, channels)
    kernel = depth_kernel[0]
    weight = point_weight[0]
    gain = bn_gain
    ids = jnp.stack([lax.axis_index("section"), lax.axis_index("dp")]).astype(jnp.int32)

    def swap(v, k):
        return lax.ppermute(v, "dp", [(i, i ^ k) for i in range(replicas)])

    riding = groups == 2 and sections % 2 == 0 and sections > 2

    def at_work(t):
        return [s for s in range(1, sections) if 0 <= t - (sections - 1 - s) < groups]

    def trade(v):
        return lax.ppermute(v, "section", [(s, s ^ 1) for s in range(sections)])

    def down(v, t):
        if t == 0 and not riding:
            return [lax.ppermute(v, "section", [(s, s - 1) for s in at_work(t)])]
        if sections % 2 == 0 and all(s % 2 for s in at_work(t)):
            return [trade(v)]
        low, high = min(at_work(t)) - 1, max(at_work(t))
        pairs = []
        for s in range(sections):
            for d in range(replicas):
                if low <= s <= high:
                    to = (s - 1 if s > low else high) * replicas + d
                else:
                    to = s * replicas + (d ^ 1)
                pairs.append((s * replicas + d, to))
        return [lax.ppermute(v, ("section", "dp"), pairs)]

    def up(v, wrap):
        pairs = [(s, (s + 1) % sections) for s in range(sections if wrap else sections - 1)]
        return lax.ppermute(v, "section", pairs)

    def pieces(v):
        return [v] + [swap(v, k) for k in range(2, replicas, 2)]

    *held, copy, x, og, kernel, weight, gain = load(ids, x, og, kernel, weight, gain, height, width, group)
    nexts = [up(copy, True)]
    depth, pre, raw = held
    later, later_raw = [], []
    for i in range(1, groups):
        depth, pre, row, copy = forward(i, x, og, kernel, weight, [depth, pre], height, width, group)
        later.append(copy)
        later_raw.append(row)
    raw = add(raw, swap(raw, 1))
    raws, starts = [pieces(raw)], [0]
    later, raw = lax.optimization_barrier((later, raw))
    if riding:
        nexts += [lax.ppermute(later[0], "section", [(s, s + 1) for s in range(1, sections - 1, 2)])]
    else:
        nexts += [up(v, False) for v in later]
        raws += [pieces(add(v, swap(v, 1))) for v in later_raw]
        starts += [0] * len(later_raw)

    recvs, tots, collected = [], [], ()
    for t in range(turns):
        last = t + 1 == turns
        *given, total, pg, dg = turn(
            t, sections, last, ids, og, raws, starts, gain, pre, x, weight, kernel, recvs, tots,
            [] if last or t == 0 else nexts, later if riding and t == 0 else [], height, width, count, group,
        )
        if last:
            keep, send = product(t, sections, ids, depth, pg, collected[2:3])
            dg, send = lax.optimization_barrier((dg, send))
            (table,) = terms(
                t, sections, last, ids, x, depth, None, pg, dg, total, collected, height, width
            )
            dg, table = lax.optimization_barrier((dg, table))
            act, gains, biases = finish(
                t, sections, ids, og, x, dg, kernel, total, recvs, collected[1:2], collected[3:], height, width
            )
        else:
            fresh, part = given
            recvs = down(fresh, t)
            if t == 0:
                part = cross(fresh, nexts[0], later_raw if riding else [])
                if riding:
                    nexts = [nexts[0], recvs[0], nexts[1]]
            other = swap(part, 1)
            part = tree(pieces(part + other))
            if t == 0 and riding:
                raws, starts = raws + [[part]], [0, 2]
            tots = down(part, t)
            collected = terms(t, sections, last, ids, x, depth, fresh, pg, dg, total, collected, height, width)
            gain, collected = lax.optimization_barrier((gain, collected))
    got = split(ids, keep, table, swap(send, 1), chips)
    recvs = [swap(v, 2 * k) for k, v in enumerate(got[1:], 1)]
    recvs, act = lax.optimization_barrier((recvs, act))
    chunk, table = merge(got[0], recvs)
    half = gather(ids, table, [chunk] + [swap(chunk, 2 * k) for k in range(1, chips)])
    point, table = widen(ids, half, swap(half, 1), widen(ids, half))
    table = table.reshape(3, 3, 1, channels).transpose(2, 0, 1, 3)
    return (act.reshape(acts.shape), point[None], table, gains, biases)


def solution(mesh):
    return jax.shard_map(
        body,
        mesh=mesh,
        in_specs=(
            P("section", None, "dp", None, None, None),
            P(None, "dp", None, None, None),
            P("section", None, None, None),
            P("section", None, None),
            P("section", None),
        ),
        out_specs=(
            P("section", None, "dp", None, None, None),
            P("section", None, None),
            P("section", None, None, None),
            P("section", None),
            P("section", None),
        ),
        check_vma=False,
    )
```
